256 devices in a mesh: row: 16 (over y, z_lo), col: 16 (over x, z_hi, core).
Axes of the slice: x: 4, y: 4, z: 8 (z_hi: 2, z_lo: 4; z = z_hi * 4 + z_lo), core: 2. Of those that a mesh axis runs over, the one named last changes fastest.
Arguments:
- features: float32 [65536, 128], P(('col', 'row')), may hold values from -6 to 6
- weight: float32 [128, 128], replicated, may hold values from -4 to 4
- bias_vector: float32 [128], replicated, may hold values from -4 to 4
- out_grad: float32 [65536, 128], P(('row', 'col')), may hold values from -6 to 6
- adj_tiles: int32 [16, 16, 128, 128, 128], P('row', 'col'), may hold values 0 or 1
- tile_slots: int32 [16, 16, 128], P('row', 'col'), may hold values from 0 to 1023, as said below
- tile_counts: int32 [16, 16], P('row', 'col'), may hold values from 17 to 128, as said below
Outputs:
- activated: float32 [65536, 128], P(('row', 'col'))
- feature_grad: float32 [65536, 128], P(('col', 'row'))
- weight_grad: float32 [128, 128], replicated
- bias_grad: float32 [128], replicated
The draws below stay inside these ranges and needn't reach their ends.
Inputs may be any that keep to these rules, and one draw needn't show every extreme that they name: `tile_slots`: each block's slots name distinct positions r * 32 + c of its 32 x 32 tiles. Some block is full in every draw; slots from tile_counts on are ignored.
All inputs are finite; a program needn't handle non-finite values. No bound on the sum of `adj_tiles` on one device may be relied on, other than what follows from the above.
Results may differ from the reference program's by a relative error of at most 0.0003.
Values sent between devices are 32-bit elements; how exact they have to be, the bound alone decides.
A program may use at most 128 MiB of HBM per device.

```python
import jax
import jax.numpy as jnp
from jax import lax

H = 128
TILE = 128
KT = 128
GRID_ROWS = 16
GRID_COLS = 16
TILE_ROWS = 32
TILE_COLS = 32
NODES = 65536


def draw_tile_slots(key, part):
    block_keys = jax.random.split(jax.random.fold_in(key, 11), GRID_ROWS * GRID_COLS)

    def one_block(block_key):
        return jax.random.permutation(block_key, TILE_ROWS * TILE_COLS)[:KT]
    return jax.vmap(one_block)(block_keys).reshape(GRID_ROWS, GRID_COLS, KT).astype(jnp.int32)


def draw_tile_counts(key, part):
    first_key, second_key = jax.random.split(jax.random.fold_in(key, 23))
    counts = jax.random.randint(first_key, (GRID_ROWS * GRID_COLS,), KT // 8 + 1, KT // 2 + 1)
    busiest = jax.random.randint(second_key, (), 0, GRID_ROWS * GRID_COLS)
    counts = jnp.where(jnp.arange(GRID_ROWS * GRID_COLS) == busiest, KT, counts)
    return counts.reshape(GRID_ROWS, GRID_COLS).astype(jnp.int32)


def touch_ends(drawn, rng, least, top_value):
    extent = drawn.shape
    place = [jax.random.randint(jax.random.fold_in(rng, axis), (), 0, extent[axis]) for axis in range(len(extent))]
    drawn = drawn.at[tuple(place)].set(least)
    longest = extent.index(max(extent))
    place[longest] = (place[longest] + 1) % extent[longest]
    return drawn.at[tuple(place)].set(top_value)


def steps_of(stream_key, dims, pieces, least, largest):
    def one(position, parts):
        draws = jax.random.uniform(jax.random.fold_in(jax.random.fold_in(stream_key, 6), position), (parts,), jnp.float32, least / len(pieces), largest / len(pieces))
        return jnp.repeat(jnp.exp(draws), dims[position] // parts).reshape((-1,) + (1,) * (len(dims) - position - 1))

    level = one(*pieces[0])
    for cut in pieces[1:]:
        level = level * one(*cut)
    return level


def gaussian(rng, extent, scale, bound, cuts=(), held_as=jnp.bfloat16):
    level = steps_of(rng, extent, cuts, -0.22, 0.18) if cuts else 1.0
    entries = jax.random.normal(rng, extent, jnp.float32) * scale * level
    return jnp.minimum(jnp.maximum(entries, -bound), bound).astype(held_as)


def setup_inputs(seed: int = 0) -> dict:
    seeds = jax.random.split(jax.random.key(seed), 8)
    features = gaussian(seeds[0], (NODES, H), 1.0, 6.0, ((0, 256),), jnp.float32)
    weight = gaussian(seeds[1], (H, H), 1.0, 4.0, (), jnp.float32)
    bias_vector = gaussian(seeds[2], (H,), 1.0, 4.0, (), jnp.float32)
    out_grad = gaussian(seeds[3], (NODES, H), 1.0, 6.0, ((0, 256),), jnp.float32)
    adj_tiles = touch_ends((jax.random.randint(seeds[4], (GRID_ROWS, GRID_COLS, KT, TILE, TILE), 0, 8) < 1).astype(jnp.int32), jax.random.fold_in(seeds[4], 1), 0, 1)
    tile_slots = draw_tile_slots(jax.random.fold_in(seeds[7], 71), 0)
    tile_counts = draw_tile_counts(jax.random.fold_in(seeds[7], 71), 0)
    return {"features": features, "weight": weight, "bias_vector": bias_vector, "out_grad": out_grad, "adj_tiles": adj_tiles, "tile_slots": tile_slots, "tile_counts": tile_counts}


def selectors(slots, slot_count, tile_rows, tile_cols):
    live_mask = (jnp.arange(slots.shape[0]) < slot_count).astype(jnp.float32)
    tile_row = slots // tile_cols
    tile_col = slots % tile_cols
    row_select = (tile_row[:, None] == jnp.arange(tile_rows)[None, :]).astype(jnp.float32)
    col_select = (tile_col[:, None] == jnp.arange(tile_cols)[None, :]).astype(jnp.float32)
    return (live_mask, row_select, col_select)

def reference(features, weight, bias_vector, out_grad, adj_tiles, tile_slots, tile_counts):
    grid_rows = adj_tiles.shape[0]
    grid_cols = adj_tiles.shape[1]
    flat_tiles = adj_tiles.reshape(grid_rows * grid_cols, KT, TILE, TILE)
    flat_slots = tile_slots.reshape(grid_rows * grid_cols, KT)
    flat_counts = tile_counts.reshape(grid_rows * grid_cols)

    def degree_parts(item):
        tile_block, slots, slot_count = item
        adjacency = tile_block.astype(jnp.float32)
        live_mask, row_select, col_select = selectors(slots, slot_count, TILE_ROWS, TILE_COLS)
        dst_partial = jnp.dot((row_select * live_mask[:, None]).T, lax.optimization_barrier(jnp.sum(adjacency, axis=2)), precision=lax.Precision.HIGHEST)
        src_partial = jnp.dot((col_select * live_mask[:, None]).T, lax.optimization_barrier(jnp.sum(adjacency, axis=1)), precision=lax.Precision.HIGHEST)
        return (dst_partial.reshape(-1), src_partial.reshape(-1))
    dst_parts, src_parts = lax.map(degree_parts, (flat_tiles, flat_slots, flat_counts))
    dst_degree = 1.0 + lax.optimization_barrier(jnp.sum(dst_parts.reshape(grid_rows, grid_cols, -1), axis=1)).reshape(-1)
    src_degree = 1.0 + lax.optimization_barrier(jnp.sum(src_parts.reshape(grid_rows, grid_cols, -1), axis=0)).reshape(-1)
    dst_scale = lax.rsqrt(dst_degree)
    src_scale = lax.rsqrt(src_degree)
    scaled = features * src_scale[:, None]
    scaled_blocks = scaled.reshape(grid_cols, TILE_COLS, TILE, H)

    def forward_row(row_index):

        def add_block(total, col_index):
            adjacency = adj_tiles[row_index, col_index].astype(jnp.float32)
            live_mask, row_select, col_select = selectors(tile_slots[row_index, col_index], tile_counts[row_index, col_index], TILE_ROWS, TILE_COLS)
            taken = jnp.einsum('kc,cbh->kbh', col_select, scaled_blocks[col_index], precision=lax.Precision.HIGHEST)
            product = jnp.einsum('kab,kbh->kah', adjacency, taken, precision=lax.Precision.HIGHEST)
            return (total + jnp.einsum('kr,kah->rah', row_select * live_mask[:, None], product, precision=lax.Precision.HIGHEST), None)
        total, unused = lax.scan(add_block, jnp.zeros((TILE_ROWS, TILE, H), jnp.float32), jnp.arange(grid_cols))
        return total
    aggregated = lax.map(forward_row, jnp.arange(grid_rows)).reshape(NODES, H) * dst_scale[:, None]
    preact = jnp.dot(aggregated, weight, precision=lax.Precision.HIGHEST) + bias_vector
    logistic = jax.nn.sigmoid(preact)
    activated = preact * logistic
    pre_grad = out_grad * logistic * (1.0 + preact * (1.0 - logistic))
    weight_grad = jnp.dot(aggregated.T, pre_grad, precision=lax.Precision.HIGHEST)
    bias_grad = lax.optimization_barrier(jnp.sum(pre_grad, axis=0))
    row_grads = jnp.dot(pre_grad, weight.T, precision=lax.Precision.HIGHEST) * dst_scale[:, None]
    row_blocks = row_grads.reshape(grid_rows, TILE_ROWS, TILE, H)

    def backward_col(col_index):

        def add_block(total, row_index):
            adjacency = adj_tiles[row_index, col_index].astype(jnp.float32)
            live_mask, row_select, col_select = selectors(tile_slots[row_index, col_index], tile_counts[row_index, col_index], TILE_ROWS, TILE_COLS)
            taken = jnp.einsum('kr,rah->kah', row_select, row_blocks[row_index], precision=lax.Precision.HIGHEST)
            product = jnp.einsum('kab,kah->kbh', adjacency, taken, precision=lax.Precision.HIGHEST)
            return (total + jnp.einsum('kc,kbh->cbh', col_select * live_mask[:, None], product, precision=lax.Precision.HIGHEST), None)
        total, unused = lax.scan(add_block, jnp.zeros((TILE_COLS, TILE, H), jnp.float32), jnp.arange(grid_rows))
        return total
    feature_grad = lax.map(backward_col, jnp.arange(grid_cols)).reshape(NODES, H) * src_scale[:, None]
    return (activated, feature_grad, weight_grad, bias_grad)
```

```python
import functools

import jax
import jax.numpy as jnp
from jax import lax
from jax.experimental import pallas as pl
from jax.experimental.pallas import tpu as pltpu
from jax.sharding import PartitionSpec as P

TILE = 128
MESH = pl.DeviceIdType.MESH
F32 = jnp.float32
BF16 = jnp.bfloat16
HIGHEST = lax.Precision.HIGHEST
VMEM_SPEC = pl.BlockSpec(memory_space=pltpu.VMEM)
CHUNK = 8
NT = (((1,), (1,)), ((), ()))
NN = (((1,), (0,)), ((), ()))
TN = (((0,), (0,)), ((), ()))


def remote(src, dst, send_sem, recv_sem, **where):
    return pltpu.make_async_remote_copy(
        src_ref=src,
        dst_ref=dst,
        send_sem=send_sem,
        recv_sem=recv_sem,
        device_id=where,
        device_id_type=MESH,
    )


def xor_peer(index, bit):
    return index + bit - 2 * bit * lax.rem(lax.div(index, bit), 2)


def greet(rows, cols):
    barrier = pltpu.get_barrier_semaphore()
    for peer in rows:
        pl.semaphore_signal(barrier, inc=1, device_id={"row": peer}, device_id_type=MESH)
    for peer in cols:
        pl.semaphore_signal(barrier, inc=1, device_id={"col": peer}, device_id_type=MESH)
    pl.semaphore_wait(barrier, len(rows) + len(cols))


def to_column(row_vector):
    spread = jnp.broadcast_to(row_vector, (TILE, TILE))
    diagonal = lax.broadcasted_iota(jnp.int32, (TILE, TILE), 0) == lax.broadcasted_iota(
        jnp.int32, (TILE, TILE), 1
    )
    return jnp.sum(jnp.where(diagonal, spread, 0.0), axis=1, keepdims=True)


def split_pair(value):
    high = value.astype(BF16)
    low = (value - high.astype(F32)).astype(BF16)
    return jnp.concatenate([high, low], axis=1)


def sort_table(slots, live, by_row):
    tile_row = jnp.floor(slots * (1.0 / 32.0))
    tile_col = slots - 32.0 * tile_row
    lane = lax.broadcasted_iota(jnp.int32, (1, TILE), 1).astype(F32)
    key = jnp.where(live, tile_row * 32.0 + tile_col if by_row else tile_col * 32.0 + tile_row, 2048.0 + lane)
    key_column = to_column(key)
    rank = jnp.sum(jnp.where(key < key_column, 1.0, 0.0), axis=1, keepdims=True)
    place = rank == lax.broadcasted_iota(jnp.int32, (TILE, TILE), 1).astype(F32)
    number = lax.broadcasted_iota(jnp.int32, (TILE, 1), 0).astype(F32)

    def moved(column):
        return jnp.sum(jnp.where(place, column, 0.0), axis=0, keepdims=True).astype(jnp.int32)

    ends = (to_column(tile_row), to_column(tile_col))
    if not by_row:
        ends = ends[::-1]
    return moved(number), moved(ends[0]), moved(ends[1])


def degree_kernel(count_ref, slots_ref, adj_ref, tiles_ref, dst_ref, src_ref, info_ref, row_sums, col_sums):
    step = pl.program_id(0)
    tiles = adj_ref[...].astype(F32).astype(BF16)
    tiles_ref[...] = tiles
    selector = (
        lax.broadcasted_iota(jnp.int32, (CHUNK, CHUNK * TILE), 1) // TILE
        == lax.broadcasted_iota(jnp.int32, (CHUNK, CHUNK * TILE), 0)
    ).astype(F32).astype(BF16)
    wide = jnp.concatenate([tiles[k] for k in range(CHUNK)], axis=1)
    tall = tiles.reshape(CHUNK * TILE, TILE)
    here = pl.ds(pl.multiple_of(step * CHUNK, CHUNK), CHUNK)
    row_sums[here, :] = lax.dot_general(selector, wide, NT, preferred_element_type=F32)
    col_sums[here, :] = lax.dot_general(selector, tall, NN, preferred_element_type=F32)

    @pl.when(step == pl.num_programs(0) - 1)
    def _():
        slots = slots_ref[...].astype(F32)
        lane = lax.broadcasted_iota(jnp.int32, (1, TILE), 1)
        live = lane < count_ref[0, 0]
        tile_row = jnp.floor(slots * (1.0 / 32.0))
        tile_col = slots - 32.0 * tile_row
        tile_number = lax.broadcasted_iota(jnp.int32, (32, TILE), 0).astype(F32)
        row_select = jnp.where(live & (tile_row == tile_number), 1.0, 0.0).astype(BF16)
        col_select = jnp.where(live & (tile_col == tile_number), 1.0, 0.0).astype(BF16)
        dst_ref[...] = jnp.dot(row_select, row_sums[...].astype(BF16), preferred_element_type=F32)
        src_ref[...] = jnp.dot(col_select, col_sums[...].astype(BF16), preferred_element_type=F32)
        info_ref[...] = jnp.zeros_like(info_ref)
        for base, by_row in ((0, True), (4, False)):
            for place, line in enumerate(sort_table(slots, live, by_row)):
                info_ref[base + place : base + place + 1, :] = line


def block_degrees(adj_tiles, slots, count):
    slot_total = adj_tiles.shape[0]
    return pl.pallas_call(
        degree_kernel,
        grid=(slot_total // CHUNK,),
        in_specs=[
            pl.BlockSpec(memory_space=pltpu.SMEM),
            pl.BlockSpec((1, TILE), lambda i: (0, 0)),
            pl.BlockSpec((CHUNK, TILE, TILE), lambda i: (i, 0, 0)),
        ],
        out_specs=[
            pl.BlockSpec((CHUNK, TILE, TILE), lambda i: (i, 0, 0)),
            pl.BlockSpec((32, TILE), lambda i: (0, 0)),
            pl.BlockSpec((32, TILE), lambda i: (0, 0)),
            pl.BlockSpec((8, TILE), lambda i: (0, 0)),
        ],
        out_shape=[
            jax.ShapeDtypeStruct((slot_total, TILE, TILE), BF16),
            jax.ShapeDtypeStruct((32, TILE), F32),
            jax.ShapeDtypeStruct((32, TILE), F32),
            jax.ShapeDtypeStruct((8, TILE), jnp.int32),
        ],
        scratch_shapes=[pltpu.VMEM((TILE, TILE), F32), pltpu.VMEM((TILE, TILE), F32)],
        name="block_degrees",
    )(count, slots, adj_tiles)


def product_kernel(dims, count_ref, info_ref, tiles_ref, pair_ref, out_ref):
    unroll = 8
    count = count_ref[0, 0]
    out_ref[...] = jnp.zeros_like(out_ref)

    def body(step, total):
        for u in range(unroll):
            k = step * unroll + u
            at = jnp.minimum(k, count - 1)
            before = jnp.maximum(at - 1, 0)
            target = info_ref[1, at]
            both = lax.dot_general(
                tiles_ref[info_ref[0, at]], pair_ref[info_ref[2, at]], dims, preferred_element_type=F32
            )
            product = both[:, :TILE] + both[:, TILE:]
            goes_on = (k > 0) & (info_ref[1, before] == target)
            joined = product + jnp.where(goes_on, total, 0.0)
            total = jnp.where(k < count, joined, total)
            out_ref[target] = total
        return total

    lax.fori_loop(0, lax.div(count + unroll - 1, unroll), body, jnp.zeros((TILE, TILE), F32))


def sparse_product(dims, count, info, tiles, pairs, name):
    return pl.pallas_call(
        functools.partial(product_kernel, dims),
        in_specs=[pl.BlockSpec(memory_space=pltpu.SMEM)] * 2 + [VMEM_SPEC] * 2,
        out_specs=VMEM_SPEC,
        out_shape=jax.ShapeDtypeStruct((32, TILE, TILE), F32),
        name=name,
    )(count, info, tiles, pairs)


LINE = ((0, 0), (1, -1), (1, 1), (2, -1), (2, 1), (3, -1), (3, 1))


def gather_kernel(
    feat_ref, src_ref, dst_ref, pair_ref, src_scale_ref, dst_scale_ref,
    held, deg_sent, deg_got, recv_sem, z_sem, y_sem, relay_sem, deg_send_sem, deg_recv_sem,
):
    row, col = lax.axis_index("row"), lax.axis_index("col")
    y, z = lax.div(row, 4), lax.rem(row, 4)
    y_up, y_down, y_far = lax.rem(y + 1, 4), lax.rem(y + 3, 4), lax.rem(y + 2, 4)
    greet(
        [lax.rem(y + d, 4) * 4 + z for d in (1, 2, 3)] + [y * 4 + lax.rem(z + d, 4) for d in (1, 2, 3)],
        [xor_peer(col, bit) for bit in (1, 2, 4, 8)],
    )

    def own(z_from, half):
        if z_from is None:
            return feat_ref.at[half]
        return held.at[y * 4 + z_from, half]

    def z_copy(z_from, first, way, half):
        block = y * 4 + z_from
        return remote(
            own(None if first else z_from, half), held.at[block, half],
            z_sem.at[z_from, way, half], recv_sem.at[block, half],
            row=y * 4 + lax.rem(z + (1 if way == 0 else 3), 4),
        )

    def y_copy(z_from, first, way, half):
        block = y * 4 + z_from
        return remote(
            own(None if first else z_from, half), held.at[block, half],
            y_sem.at[z_from, way, half], recv_sem.at[block, half],
            row=(y_up if way == 0 else y_down) * 4 + z,
        )

    def relay_copy(z_from, half):
        block = (y_down if half == 0 else y_up) * 4 + z_from
        return remote(
            held.at[block, half], held.at[block, half],
            relay_sem.at[z_from, half], recv_sem.at[block, half],
            row=(y_up if half == 0 else y_down) * 4 + z,
        )

    def arrived(block, half):
        remote(
            held.at[block, half], held.at[block, half], relay_sem.at[0, half], recv_sem.at[block, half],
            row=y_up * 4 + z,
        ).wait_recv()

    def here(distance, sign):
        return (z + sign * distance >= 0) & (z + sign * distance <= 3)

    def on_way(distance, sign, action):
        z_from = z + sign * distance
        for way, goes in ((0, z < 3), (1, z > 0)):
            if distance and (way == 0) != (sign < 0):
                continue

            @pl.when(goes)
            def _():
                for half in (0, 1):
                    action(z_copy(z_from, distance == 0, way, half))

    def column_step(distance, sign):
        z_from = z + sign * distance
        if distance:
            for half in (0, 1):
                arrived(y * 4 + z_from, half)
        for half in (0, 1):
            for way in (0, 1):
                y_copy(z_from, distance == 0, way, half).start()
        on_way(distance, sign, lambda copy: copy.start())

    def relay_step(distance, sign):
        z_from = z + sign * distance
        for half in (0, 1):
            arrived((y_down if half == 0 else y_up) * 4 + z_from, half)
            relay_copy(z_from, half).start()

    def degree_copy(which, step):
        source = (src_ref, dst_ref)[which] if step == 0 else deg_sent.at[which, step - 1]
        where = {("row", "col")[which]: xor_peer((row, col)[which], 1 << step)}
        return remote(
            source, deg_got.at[which, step], deg_send_sem.at[which, step], deg_recv_sem.at[which, step], **where
        )

    def degree_step(step):
        for which in (0, 1):
            copy = degree_copy(which, step)
            copy.wait_recv()
            source = (src_ref, dst_ref)[which] if step == 0 else deg_sent.at[which, step - 1]
            deg_sent[which, step] = source[...] + deg_got[which, step]
            if step < 3:
                degree_copy(which, step + 1).start()

    for which in (0, 1):
        degree_copy(which, 0).start()
    column_step(0, 0)
    held[row] = feat_ref[...]
    degree_step(0)
    for place, (distance, sign) in enumerate(LINE[1:]):
        pl.when(here(distance, sign))(functools.partial(column_step, distance, sign))
        before = LINE[place]
        pl.when(here(*before))(functools.partial(relay_step, *before))
        if place in (1, 3, 5):
            degree_step(1 + place // 2)
    pl.when(here(*LINE[-1]))(functools.partial(relay_step, *LINE[-1]))

    src_scale = lax.rsqrt(1.0 + deg_sent[0, 3])
    src_scale_ref[...] = src_scale
    dst_scale_ref[...] = lax.rsqrt(1.0 + deg_sent[1, 3])

    def settle(block):
        for half in (0, 1):
            tile = 2 * block + half
            scale = to_column(src_scale_ref[pl.ds(tile, 1), :])
            pair_ref[tile] = split_pair(held[block, half] * scale)

    for z_from in range(4):
        settle(y * 4 + z_from)

    def last_step(distance, sign):
        z_from = z + sign * distance
        arrived(y_down * 4 + z_from, 1)
        settle(y_down * 4 + z_from)
        arrived(y_up * 4 + z_from, 0)
        settle(y_up * 4 + z_from)

    def far_step(distance, sign):
        z_from = z + sign * distance
        arrived(y_far * 4 + z_from, 0)
        arrived(y_far * 4 + z_from, 1)
        settle(y_far * 4 + z_from)

    def send_step(distance, sign):
        z_from = z + sign * distance
        for half in (0, 1):
            for way in (0, 1):
                y_copy(z_from, distance == 0, way, half).wait_send()
            relay_copy(z_from, half).wait_send()
        on_way(distance, sign, lambda copy: copy.wait_send())

    for action in (last_step, far_step, send_step):
        for item in LINE:
            pl.when(here(*item))(functools.partial(action, *item))
    for which in (0, 1):
        for step in range(4):
            degree_copy(which, step).wait_send()


def gather_features(features, src_part, dst_part):
    dma = pltpu.SemaphoreType.DMA
    return pl.pallas_call(
        gather_kernel,
        in_specs=[VMEM_SPEC] * 3,
        out_specs=[VMEM_SPEC] * 3,
        out_shape=[
            jax.ShapeDtypeStruct((32, TILE, 2 * TILE), BF16),
            jax.ShapeDtypeStruct((32, TILE), F32),
            jax.ShapeDtypeStruct((32, TILE), F32),
        ],
        scratch_shapes=[
            pltpu.VMEM((16, 2, TILE, TILE), F32),
            pltpu.VMEM((2, 4, 32, TILE), F32),
            pltpu.VMEM((2, 4, 32, TILE), F32),
            dma((16, 2)),
            dma((4, 2, 2)),
            dma((4, 2, 2)),
            dma((4, 2)),
            dma((2, 4)),
            dma((2, 4)),
        ],
        compiler_params=pltpu.CompilerParams(collective_id=0, has_side_effects=True),
        name="gather_features",
    )(features.reshape(2, TILE, TILE), src_part, dst_part)


WROWS = 72


def layer_kernel(
    part_ref, w_ref, b_ref, grad_ref, scale_ref, act_ref, pair_ref, wsum_ref,
    sib_got, ring_a, ring_b, from_left, from_right, z_sent, z_got, held, wgrad, w_sent, w_got,
    sib_ssem, sib_rsem, far_ssem, far_rsem, near_ssem, near_rsem, z_ssem, z_rsem,
    recv_sem, zg_sem, xg_sem, relay_sem, sg_sem, w_ssem, w_rsem,
):
    col = lax.axis_index("col")
    x, zh, core = lax.div(col, 4), lax.rem(lax.div(col, 2), 2), lax.rem(col, 2)
    x_up, x_down, x_far = lax.rem(x + 1, 4), lax.rem(x + 3, 4), lax.rem(x + 2, 4)
    sibling = col + 1 - 2 * core
    z_peer = col + 2 - 4 * zh
    up, down = x_up * 4 + zh * 2 + core, x_down * 4 + zh * 2 + core
    greet([], [sibling, z_peer, up, down, x_far * 4 + zh * 2 + core])

    def sib_copy(place, which):
        target = (x_far, x_up, x_down, x)[place]
        half_z = 1 - zh if which == 0 else zh
        return remote(
            part_ref.at[target * 4 + half_z * 2 + 1 - core], sib_got.at[place, which],
            sib_ssem.at[place, which], sib_rsem.at[place, which], col=sibling,
        )

    def far_copy(which, way):
        return remote(
            sib_got.at[0, which, way], (ring_a, ring_b)[way].at[which],
            far_ssem.at[which, way], far_rsem.at[which, way], col=(up, down)[way],
        )

    def near_copy(which, way, half):
        return remote(
            sib_got.at[1 + way, which, half], (from_left, from_right)[way].at[which, half],
            near_ssem.at[which, way, half], near_rsem.at[which, way, half], col=(up, down)[way],
        )

    def z_copy(half):
        return remote(z_sent.at[half], z_got.at[half], z_ssem.at[half], z_rsem.at[half], col=z_peer)

    def join(place, which):
        target = (x_far, x_up, x_down, x)[place]
        half_z = 1 - zh if which == 0 else zh
        sib_copy(place, which).wait_recv()
        sib_got[place, which] += part_ref[target * 4 + half_z * 2 + core]

    for which in (0, 1):
        for place in range(4):
            sib_copy(place, which).start()
    for which in (0, 1):
        join(0, which)
        for way in (0, 1):
            far_copy(which, way).start()
        for way in (0, 1):
            join(1 + way, which)
            near_copy(which, way, 1 - way).start()
    for which in (0, 1):
        for way in (0, 1):
            far_copy(which, way).wait_recv()
            sib_got[1 + way, which, way] += (ring_a, ring_b)[way][which]
            near_copy(which, way, way).start()
    for which in (0, 1):
        join(3, which)
        for half in (1, 0):
            for way in (0, 1):
                near_copy(which, way, half).wait_recv()
            total = sib_got[3, which, half] + from_left[which, half] + from_right[which, half]
            if which == 0:
                z_sent[half] = total
                z_copy(half).start()
            else:
                sib_got[3, which, half] = total
    for half in (0, 1):
        z_copy(half).wait_recv()

    scales, pre_grads, rows = [], [], []
    for half in (0, 1):
        scale = to_column(scale_ref[pl.ds(2 * col + half, 1), :])
        rows.append((sib_got[3, 1, half] + z_got[half]) * scale)
        scales.append(scale)
    aggregated = jnp.concatenate(rows, axis=0)
    scale = jnp.concatenate(scales, axis=0)
    preact = jnp.dot(aggregated, w_ref[...], precision=HIGHEST, preferred_element_type=F32) + b_ref[...]
    logistic = 1.0 / (1.0 + jnp.exp(-preact))
    act_ref[...] = preact * logistic
    pre_grad = grad_ref[...] * logistic * (1.0 + preact * (1.0 - logistic))
    back = lax.dot_general(pre_grad, w_ref[...], NT, precision=HIGHEST, preferred_element_type=F32) * scale
    held[col, 0] = back[:TILE]
    held[col, 1] = back[TILE:]

    def spread_z(half):
        return remote(
            held.at[col, half], held.at[col, half], zg_sem.at[half], recv_sem.at[col, half], col=z_peer
        )

    def spread_x(which, way, half):
        half_z = zh if which == 0 else 1 - zh
        block = x * 4 + half_z * 2 + core
        return remote(
            held.at[block, half], held.at[block, half], xg_sem.at[which, way, half], recv_sem.at[block, half],
            col=(up, down)[way],
        )

    def relay_x(which, half):
        half_z = zh if which == 0 else 1 - zh
        block = (x_down if half == 0 else x_up) * 4 + half_z * 2 + core
        return remote(
            held.at[block, half], held.at[block, half], relay_sem.at[which, half], recv_sem.at[block, half],
            col=(up, down)[half],
        )

    def spread_sib(place, which, half):
        target = (x, x_up, x_down, x_far)[place]
        half_z = zh if which == 0 else 1 - zh
        block = target * 4 + half_z * 2 + core
        return remote(
            held.at[block, half], held.at[block, half], sg_sem.at[place, which, half], recv_sem.at[block, half],
            col=sibling,
        )

    def arrived(block, half):
        remote(
            held.at[block, half], held.at[block, half], zg_sem.at[half], recv_sem.at[block, half], col=sibling
        ).wait_recv()

    def settle(block, half):
        pair_ref[2 * block + half] = split_pair(held[block, half])

    for half in (0, 1):
        spread_z(half).start()
    for half in (0, 1):
        for way in (0, 1):
            spread_x(0, way, half).start()
    for half in (0, 1):
        spread_sib(0, 0, half).start()

    wgrad[0:TILE, :] = lax.dot_general(aggregated, pre_grad, TN, precision=HIGHEST, preferred_element_type=F32)
    first_row = lax.broadcasted_iota(jnp.int32, (16, TILE), 0) == 0
    wgrad[TILE : TILE + 16, :] = jnp.where(first_row, jnp.sum(pre_grad, axis=0, keepdims=True), 0.0)

    def w_rows(which):
        return pl.ds(pl.multiple_of(which * WROWS, 8), WROWS)

    def w_copy(step):
        if step == 0:
            return remote(
                wgrad.at[w_rows(1 - core)], w_got.at[0], w_ssem.at[0], w_rsem.at[0], col=sibling
            )
        peer = xor_peer(col, 1 << step)
        return remote(w_sent.at[step - 1], w_got.at[step], w_ssem.at[step], w_rsem.at[step], col=peer)

    def w_step(step):
        w_copy(step).wait_recv()
        mine = wgrad[w_rows(core), :] if step == 0 else w_sent[step - 1]
        total = mine + w_got[step]
        if step < 3:
            w_sent[step] = total
            w_copy(step + 1).start()
        else:
            wsum_ref[...] = total

    def relay(which):
        half_z = zh if which == 0 else 1 - zh
        for half in (0, 1):
            side = x_down if half == 0 else x_up
            arrived(side * 4 + half_z * 2 + core, half)
            relay_x(which, half).start()
            spread_sib((2, 1)[half], which, half).start()

    def near_rest(which):
        half_z = zh if which == 0 else 1 - zh
        for half in (0, 1):
            side = x_up if half == 0 else x_down
            arrived(side * 4 + half_z * 2 + core, half)
            spread_sib((1, 2)[half], which, half).start()

    def far_rest(which):
        half_z = zh if which == 0 else 1 - zh
        for half in (0, 1):
            arrived(x_far * 4 + half_z * 2 + core, half)
            spread_sib(3, which, half).start()

    w_copy(0).start()
    relay(0)
    near_rest(0)
    w_step(0)
    other = x * 4 + (1 - zh) * 2 + core
    for half in (0, 1):
        arrived(other, half)
        for way in (0, 1):
            spread_x(1, way, half).start()
        spread_sib(0, 1, half).start()
    far_rest(0)
    w_step(1)
    for side in (x, x_up, x_down, x_far):
        for half in (0, 1):
            settle(side * 4 + zh * 2 + core, half)
    relay(1)
    near_rest(1)
    w_step(2)
    for side in (x, x_up, x_down, x_far):
        for half in (0, 1):
            block = side * 4 + zh * 2 + 1 - core
            arrived(block, half)
            settle(block, half)
    far_rest(1)
    w_step(3)
    for side in (x, x_up, x_down, x_far):
        for half in (0, 1):
            settle(side * 4 + (1 - zh) * 2 + core, half)
    for side in (x, x_up, x_down, x_far):
        for half in (0, 1):
            block = side * 4 + (1 - zh) * 2 + 1 - core
            arrived(block, half)
            settle(block, half)

    for which in (0, 1):
        for place in range(4):
            sib_copy(place, which).wait_send()
            for half in (0, 1):
                spread_sib(place, which, half).wait_send()
        for way in (0, 1):
            far_copy(which, way).wait_send()
            relay_x(which, way).wait_send()
            for half in (0, 1):
                near_copy(which, way, half).wait_send()
                spread_x(which, way, half).wait_send()
    for half in (0, 1):
        z_copy(half).wait_send()
        spread_z(half).wait_send()
    for step in range(4):
        w_copy(step).wait_send()


def dense_layer(part, weight, bias_vector, out_grad, dst_scale):
    dma = pltpu.SemaphoreType.DMA
    half = (TILE, TILE)
    return pl.pallas_call(
        layer_kernel,
        in_specs=[VMEM_SPEC] * 5,
        out_specs=[VMEM_SPEC] * 3,
        out_shape=[
            jax.ShapeDtypeStruct((2 * TILE, TILE), F32),
            jax.ShapeDtypeStruct((32, TILE, 2 * TILE), BF16),
            jax.ShapeDtypeStruct((WROWS, TILE), F32),
        ],
        scratch_shapes=[
            pltpu.VMEM((4, 2, 2) + half, F32),
            pltpu.VMEM((2,) + half, F32),
            pltpu.VMEM((2,) + half, F32),
            pltpu.VMEM((2, 2) + half, F32),
            pltpu.VMEM((2, 2) + half, F32),
            pltpu.VMEM((2,) + half, F32),
            pltpu.VMEM((2,) + half, F32),
            pltpu.VMEM((16, 2) + half, F32),
            pltpu.VMEM((2 * WROWS, TILE), F32),
            pltpu.VMEM((3, WROWS, TILE), F32),
            pltpu.VMEM((4, WROWS, TILE), F32),
            dma((4, 2)), dma((4, 2)), dma((2, 2)), dma((2, 2)), dma((2, 2, 2)), dma((2, 2, 2)), dma((2,)), dma((2,)),
            dma((16, 2)), dma((2,)), dma((2, 2, 2)), dma((2, 2)), dma((4, 2, 2)), dma((4,)), dma((4,)),
        ],
        compiler_params=pltpu.CompilerParams(collective_id=1, has_side_effects=True),
        name="dense_layer",
    )(part.reshape((16, 2) + half), weight, bias_vector.reshape(1, TILE), out_grad, dst_scale)


def scatter_kernel(
    part_ref, wsum_ref, scale_ref, grad_ref, wgrad_ref,
    staged_a, staged_b, ring_a, ring_b, from_down, from_up, total, line_up, line_down, w_sent, w_got, w_all,
    far_ssem, far_rsem, near_ssem, near_rsem, line_ssem, line_rsem, w_ssem, w_rsem,
):
    row, col = lax.axis_index("row"), lax.axis_index("col")
    y, z = lax.div(row, 4), lax.rem(row, 4)
    core = lax.rem(col, 2)
    y_up, y_down, y_far = lax.rem(y + 1, 4), lax.rem(y + 3, 4), lax.rem(y + 2, 4)
    sibling = col + 1 - 2 * core
    greet(
        [lax.rem(y + d, 4) * 4 + z for d in (1, 2, 3)] + [y * 4 + lax.rem(z + d, 4) for d in (1, 2, 3)],
        [sibling],
    )
    up, down = y_up * 4 + z, y_down * 4 + z

    def here(distance, sign):
        return (z + sign * distance >= 0) & (z + sign * distance <= 3)

    def far_copy(zb, way):
        return remote(
            part_ref.at[y_far * 4 + zb, way], (ring_a, ring_b)[way].at[zb],
            far_ssem.at[zb, way], far_rsem.at[zb, way], row=(up, down)[way],
        )

    def near_copy(zb, way, half):
        block = (y_up, y_down)[way] * 4 + zb
        source = (staged_a, staged_b)[way].at[zb] if half == way else part_ref.at[block, half]
        return remote(
            source, (from_down, from_up)[way].at[zb, half],
            near_ssem.at[zb, way, half], near_rsem.at[zb, way, half], row=(up, down)[way],
        )

    def line_copy(zb, way, half):
        return remote(
            total.at[zb, half], (line_up, line_down)[way].at[zb, half],
            line_ssem.at[zb, half], line_rsem.at[zb, way, half], row=y * 4 + lax.rem(z + (1 if way == 0 else 3), 4),
        )

    def w_copy(step):
        if step == 4:
            return remote(w_sent.at[3], w_all, w_ssem.at[4], w_rsem.at[4], col=sibling)
        source = wsum_ref if step == 0 else w_sent.at[step - 1]
        return remote(source, w_got.at[step], w_ssem.at[step], w_rsem.at[step], row=xor_peer(row, 1 << step))

    def w_step(step):
        w_copy(step).wait_recv()
        source = wsum_ref if step == 0 else w_sent.at[step - 1]
        w_sent[step] = source[...] + w_got[step]
        w_copy(step + 1).start()

    def open_step(distance, sign):
        zb = z + sign * distance
        for way in (0, 1):
            far_copy(zb, way).start()
        for way in (0, 1):
            near_copy(zb, way, 1 - way).start()

    def relay_step(distance, sign):
        zb = z + sign * distance
        for way in (0, 1):
            far_copy(zb, way).wait_recv()
            block = (y_up, y_down)[way] * 4 + zb
            (staged_a, staged_b)[way][zb] = part_ref[block, way] + (ring_a, ring_b)[way][zb]
            near_copy(zb, way, way).start()

    def close_step(distance, sign):
        zb = z + sign * distance
        for half in (0, 1):
            for way in (0, 1):
                near_copy(zb, way, half).wait_recv()
            total[zb, half] = part_ref[y * 4 + zb, half] + from_down[zb, half] + from_up[zb, half]

        def collect(way):
            for half in (0, 1):
                line_copy(zb, way, half).wait_recv()
                total[zb, half] += (line_up, line_down)[way][zb, half]

        if distance == 0:
            pl.when(z > 0)(functools.partial(collect, 0))
            pl.when(z < 3)(functools.partial(collect, 1))
        else:
            way = 0 if sign > 0 else 1
            pl.when(z > 0 if way == 0 else z < 3)(functools.partial(collect, way))
            for half in (0, 1):
                line_copy(zb, way, half).start()

    def send_step(distance, sign):
        zb = z + sign * distance
        for way in (0, 1):
            far_copy(zb, way).wait_send()
            for half in (0, 1):
                near_copy(zb, way, half).wait_send()
        if distance:
            for half in (0, 1):
                line_copy(zb, 0 if sign > 0 else 1, half).wait_send()

    backwards = LINE[::-1]
    for item in backwards:
        pl.when(here(*item))(functools.partial(open_step, *item))
    w_copy(0).start()
    for place, item in enumerate(backwards):
        pl.when(here(*item))(functools.partial(relay_step, *item))
        if place >= 1:
            before = backwards[place - 1]
            pl.when(here(*before))(functools.partial(close_step, *before))
        if place in (2, 3, 4, 6):
            w_step((2, 3, 4, 6).index(place))
    close_step(*backwards[-1])

    for half in (0, 1):
        scale = to_column(scale_ref[pl.ds(2 * row + half, 1), :])
        grad_ref[pl.ds(half * TILE, TILE), :] = total[z, half] * scale
    w_copy(4).wait_recv()
    wgrad_ref[pl.ds(pl.multiple_of(core * WROWS, 8), WROWS), :] = w_sent[3]
    wgrad_ref[pl.ds(pl.multiple_of((1 - core) * WROWS, 8), WROWS), :] = w_all[...]
    for item in backwards:
        pl.when(here(*item))(functools.partial(send_step, *item))
    for step in range(5):
        w_copy(step).wait_send()


def scatter_gradients(part, wsum, src_scale):
    dma = pltpu.SemaphoreType.DMA
    half = (TILE, TILE)
    return pl.pallas_call(
        scatter_kernel,
        in_specs=[VMEM_SPEC] * 3,
        out_specs=[VMEM_SPEC] * 2,
        out_shape=[
            jax.ShapeDtypeStruct((2 * TILE, TILE), F32),
            jax.ShapeDtypeStruct((2 * WROWS, TILE), F32),
        ],
        scratch_shapes=[
            pltpu.VMEM((4,) + half, F32),
            pltpu.VMEM((4,) + half, F32),
            pltpu.VMEM((4,) + half, F32),
            pltpu.VMEM((4,) + half, F32),
            pltpu.VMEM((4, 2) + half, F32),
            pltpu.VMEM((4, 2) + half, F32),
            pltpu.VMEM((4, 2) + half, F32),
            pltpu.VMEM((4, 2) + half, F32),
            pltpu.VMEM((4, 2) + half, F32),
            pltpu.VMEM((4, WROWS, TILE), F32),
            pltpu.VMEM((4, WROWS, TILE), F32),
            pltpu.VMEM((WROWS, TILE), F32),
            dma((4, 2)), dma((4, 2)), dma((4, 2, 2)), dma((4, 2, 2)), dma((4, 2)), dma((4, 2, 2)), dma((5,)), dma((5,)),
        ],
        compiler_params=pltpu.CompilerParams(collective_id=2, has_side_effects=True),
        name="scatter_gradients",
    )(part.reshape((16, 2) + half), wsum, src_scale)


def local(features, weight, bias_vector, out_grad, adj_tiles, tile_slots, tile_counts):
    tiles, dst_part, src_part, info = block_degrees(adj_tiles[0, 0], tile_slots[0], tile_counts)
    pairs, src_scale, dst_scale = gather_features(features, src_part, dst_part)
    part = sparse_product(NN, tile_counts, info[:4], tiles, pairs, "forward_product")
    activated, grad_pairs, wsum = dense_layer(part, weight, bias_vector, out_grad, dst_scale)
    back = sparse_product(TN, tile_counts, info[4:], tiles, grad_pairs, "backward_product")
    feature_grad, wgrad = scatter_gradients(back, wsum, src_scale)
    return activated, feature_grad, wgrad[:TILE], wgrad[TILE]


def solution(mesh):
    return jax.shard_map(
        local,
        mesh=mesh,
        in_specs=(
            P(("col", "row"), None),
            P(),
            P(),
            P(("row", "col"), None),
            P("row", "col", None, None, None),
            P("row", "col", None),
            P("row", "col"),
        ),
        out_specs=(P(("row", "col"), None), P(("col", "row"), None), P(), P()),
        check_vma=False,
    )
```

```python
import functools

import jax
import jax.numpy as jnp
from jax import lax
from jax.experimental import pallas as pl
from jax.experimental.pallas import tpu as pltpu
from jax.sharding import PartitionSpec as P

TILE = 128
MESH = pl.DeviceIdType.MESH
F32 = jnp.float32
BF16 = jnp.bfloat16
HIGHEST = lax.Precision.HIGHEST
VMEM_SPEC = pl.BlockSpec(memory_space=pltpu.VMEM)
CHUNK = 8
BY_WAY = ((0, 0), (1, 1), (0, 1), (1, 0))
LIMIT = 24 << 20
NT = (((1,), (1,)), ((), ()))
NN = (((1,), (0,)), ((), ()))
TN = (((0,), (0,)), ((), ()))


def remote(src, dst, send_sem, recv_sem, **where):
    return pltpu.make_async_remote_copy(
        src_ref=src,
        dst_ref=dst,
        send_sem=send_sem,
        recv_sem=recv_sem,
        device_id=where,
        device_id_type=MESH,
    )


def xor_peer(index, bit):
    return index + bit - 2 * bit * lax.rem(lax.div(index, bit), 2)


def greet(rows, cols):
    barrier = pltpu.get_barrier_semaphore()
    for peer in rows:
        pl.semaphore_signal(barrier, inc=1, device_id={"row": peer}, device_id_type=MESH)
    for peer in cols:
        pl.semaphore_signal(barrier, inc=1, device_id={"col": peer}, device_id_type=MESH)
    return lambda: pl.semaphore_wait(barrier, len(rows) + len(cols))


def to_column(row_vector):
    spread = jnp.broadcast_to(row_vector, (TILE, TILE))
    diagonal = lax.broadcasted_iota(jnp.int32, (TILE, TILE), 0) == lax.broadcasted_iota(
        jnp.int32, (TILE, TILE), 1
    )
    return jnp.sum(jnp.where(diagonal, spread, 0.0), axis=1, keepdims=True)


def split_pair(value):
    high = value.astype(BF16)
    low = (value - high.astype(F32)).astype(BF16)
    return jnp.concatenate([high, low], axis=1)


def sort_table(slots, live, by_row):
    tile_row = jnp.floor(slots * (1.0 / 32.0))
    tile_col = slots - 32.0 * tile_row
    lane = lax.broadcasted_iota(jnp.int32, (1, TILE), 1).astype(F32)
    key = jnp.where(live, tile_row * 32.0 + tile_col if by_row else tile_col * 32.0 + tile_row, 2048.0 + lane)
    key_column = to_column(key)
    rank = jnp.sum(jnp.where(key < key_column, 1.0, 0.0), axis=1, keepdims=True)
    place = rank == lax.broadcasted_iota(jnp.int32, (TILE, TILE), 1).astype(F32)
    number = lax.broadcasted_iota(jnp.int32, (TILE, 1), 0).astype(F32)

    def moved(column):
        return jnp.sum(jnp.where(place, column, 0.0), axis=0, keepdims=True).astype(jnp.int32)

    ends = (to_column(tile_row), to_column(tile_col))
    if not by_row:
        ends = ends[::-1]
    return moved(number), moved(ends[0]), moved(ends[1])


def product_kernel(dims, count_ref, info_ref, tiles_ref, pair_ref, out_ref):
    unroll = 8
    count = count_ref[0, 0]
    out_ref[...] = jnp.zeros_like(out_ref)

    def body(step, total):
        for u in range(unroll):
            k = step * unroll + u
            at = jnp.minimum(k, count - 1)
            before = jnp.maximum(at - 1, 0)
            target = info_ref[1, at]
            both = lax.dot_general(
                tiles_ref[info_ref[0, at]], pair_ref[info_ref[2, at]], dims, preferred_element_type=F32
            )
            product = both[:, :TILE] + both[:, TILE:]
            goes_on = (k > 0) & (info_ref[1, before] == target)
            joined = product + jnp.where(goes_on, total, 0.0)
            total = jnp.where(k < count, joined, total)
            out_ref[target] = total
        return total

    lax.fori_loop(0, lax.div(count + unroll - 1, unroll), body, jnp.zeros((TILE, TILE), F32))


def sparse_product(dims, count, info, tiles, pairs, name):
    return pl.pallas_call(
        functools.partial(product_kernel, dims),
        in_specs=[pl.BlockSpec(memory_space=pltpu.SMEM)] * 2 + [VMEM_SPEC] * 2,
        out_specs=VMEM_SPEC,
        out_shape=jax.ShapeDtypeStruct((32, TILE, TILE), F32),
        compiler_params=pltpu.CompilerParams(vmem_limit_bytes=LIMIT),
        name=name,
    )(count, info, tiles, pairs)


OUTWARD = ((0, 1, 2, 3), (1, 0, 2, 3), (2, 1, 3, 0), (3, 2, 1, 0))
INWARD = tuple(order[::-1] for order in OUTWARD)


def in_order(orders, place, z):
    low, high = lax.rem(z, 2), lax.div(z, 2)
    v = [orders[k][place] for k in range(4)]
    return v[0] + (v[1] - v[0]) * low + (v[2] - v[0]) * high + (v[3] - v[2] - v[1] + v[0]) * low * high


def gather_kernel(
    count_ref, slots_ref, feat_ref, adj_ref,
    tiles_ref, pair_ref, src_scale_ref, dst_scale_ref, forward_info_ref, backward_info_ref,
    adj_got, row_sums, col_sums, parts, held, deg_sent, deg_got,
    feat_sem, adj_sem, recv_sem, z_sem, y_sem, relay_sem, deg_send_sem, deg_recv_sem,
):
    chunks = adj_ref.shape[0] // CHUNK
    row, col = lax.axis_index("row"), lax.axis_index("col")
    y, z = lax.div(row, 4), lax.rem(row, 4)
    y_up, y_down, y_far = lax.rem(y + 1, 4), lax.rem(y + 3, 4), lax.rem(y + 2, 4)
    wait_for_all = greet(
        [lax.rem(y + d, 4) * 4 + z for d in (1, 2, 3)] + [y * 4 + lax.rem(z + d, 4) for d in (1, 2, 3)],
        [xor_peer(col, bit) for bit in (1, 2, 4, 8)],
    )

    def adj_copy(chunk):
        here = pl.ds(pl.multiple_of(chunk * CHUNK, CHUNK), CHUNK)
        return pltpu.make_async_copy(adj_ref.at[here], adj_got.at[here], adj_sem.at[chunk])

    feat_copy = pltpu.make_async_copy(feat_ref, held.at[row], feat_sem)
    feat_copy.start()
    for chunk in range(chunks):
        adj_copy(chunk).start()

    ones = jnp.ones((TILE, TILE), F32).astype(BF16)
    diagonal = lax.broadcasted_iota(jnp.int32, (TILE, TILE), 0) == lax.broadcasted_iota(
        jnp.int32, (TILE, TILE), 1
    )

    def degree_chunks(first, last):
        def body(chunk, carry):
            adj_copy(chunk).wait()
            for k in range(CHUNK):
                slot = chunk * CHUNK + k
                tile = adj_got[slot].astype(F32)
                narrow = tile.astype(BF16)
                tiles_ref[slot] = narrow
                col_sums[pl.ds(slot, 1), :] = jnp.sum(tile, axis=0, keepdims=True)
                sums = jnp.dot(narrow, ones, preferred_element_type=F32)
                row_sums[pl.ds(slot, 1), :] = jnp.sum(jnp.where(diagonal, sums, 0.0), axis=0, keepdims=True)
            return carry

        lax.fori_loop(first, last, body, 0)

    slots = slots_ref[...].astype(F32)
    live = lax.broadcasted_iota(jnp.int32, (1, TILE), 1) < count_ref[0, 0]

    def degree_parts():
        tile_row = jnp.floor(slots * (1.0 / 32.0))
        tile_col = slots - 32.0 * tile_row
        tile_number = lax.broadcasted_iota(jnp.int32, (32, TILE), 0).astype(F32)
        row_select = jnp.where(live & (tile_row == tile_number), 1.0, 0.0).astype(BF16)
        col_select = jnp.where(live & (tile_col == tile_number), 1.0, 0.0).astype(BF16)
        parts[0] = jnp.dot(col_select, col_sums[...].astype(BF16), preferred_element_type=F32)
        parts[1] = jnp.dot(row_select, row_sums[...].astype(BF16), preferred_element_type=F32)

    def z_copy(z_from, way, half):
        block = y * 4 + z_from
        return remote(
            held.at[block, half], held.at[block, half],
            z_sem.at[z_from, way, half], recv_sem.at[block, half],
            row=y * 4 + lax.rem(z + (1 if way == 0 else 3), 4),
        )

    def y_copy(z_from, way, half):
        block = y * 4 + z_from
        return remote(
            held.at[block, half], held.at[block, half],
            y_sem.at[z_from, way, half], recv_sem.at[block, half],
            row=(y_up if way == 0 else y_down) * 4 + z,
        )

    def relay_copy(z_from, half):
        block = (y_down if half == 0 else y_up) * 4 + z_from
        return remote(
            held.at[block, half], held.at[block, half],
            relay_sem.at[z_from, half], recv_sem.at[block, half],
            row=(y_up if half == 0 else y_down) * 4 + z,
        )

    def arrived(block, half):
        remote(
            held.at[block, half], held.at[block, half], relay_sem.at[0, half], recv_sem.at[block, half],
            row=y_up * 4 + z,
        ).wait_recv()

    def on_line(place, action):
        z_from = in_order(OUTWARD, place, z)
        for way in (0, 1):
            goes = z < 3 if way == 0 else z > 0
            if place:
                goes = goes & (z_from < z if way == 0 else z_from > z)

            @pl.when(goes)
            def _():
                for half in (0, 1):
                    action(z_copy(z_from, way, half))

    def column_step(place):
        z_from = in_order(OUTWARD, place, z)
        if place:
            for half in (0, 1):
                arrived(y * 4 + z_from, half)
        on_line(place, lambda copy: copy.start())
        for way, half in BY_WAY:
            y_copy(z_from, way, half).start()

    def relay_step(place):
        z_from = in_order(OUTWARD, place, z)
        for half in (0, 1):
            arrived((y_down if half == 0 else y_up) * 4 + z_from, half)
            relay_copy(z_from, half).start()

    def degree_source(which, step):
        return parts.at[which] if step == 0 else deg_sent.at[which, step - 1]

    def degree_copy(which, step):
        where = {("row", "col")[which]: xor_peer((row, col)[which], 1 << step)}
        return remote(
            degree_source(which, step), deg_got.at[which, step],
            deg_send_sem.at[which, step], deg_recv_sem.at[which, step], **where
        )

    def degree_step(step):
        for which in (0, 1):
            degree_copy(which, step).wait_recv()
            deg_sent[which, step] = degree_source(which, step)[...] + deg_got[which, step]
            if step < 3:
                degree_copy(which, step + 1).start()

    degree_chunks(0, chunks // 2)
    feat_copy.wait()
    wait_for_all()
    column_step(0)
    degree_chunks(chunks // 2, chunks)
    degree_parts()
    for which in (0, 1):
        degree_copy(which, 0).start()
    relay_step(0)
    column_step(1)
    degree_step(0)
    relay_step(1)
    column_step(2)
    degree_step(1)
    relay_step(2)
    column_step(3)
    degree_step(2)
    for info_ref, by_row in ((forward_info_ref, True), (backward_info_ref, False)):
        for place, line in enumerate(sort_table(slots, live, by_row)):
            info_ref[place : place + 1, :] = line
    relay_step(3)
    degree_step(3)

    src_scale_ref[...] = lax.rsqrt(1.0 + deg_sent[0, 3])
    dst_scale_ref[...] = lax.rsqrt(1.0 + deg_sent[1, 3])

    def settle(block):
        for half in (0, 1):
            tile = 2 * block + half
            scale = to_column(src_scale_ref[pl.ds(tile, 1), :])
            pair_ref[tile] = split_pair(held[block, half] * scale)

    for place in range(4):
        settle(y * 4 + in_order(OUTWARD, place, z))
    for place in range(4):
        z_from = in_order(OUTWARD, place, z)
        arrived(y_down * 4 + z_from, 1)
        settle(y_down * 4 + z_from)
        arrived(y_up * 4 + z_from, 0)
        settle(y_up * 4 + z_from)
    for place in range(4):
        z_from = in_order(OUTWARD, place, z)
        arrived(y_far * 4 + z_from, 0)
        arrived(y_far * 4 + z_from, 1)
        settle(y_far * 4 + z_from)
    for place in range(4):
        z_from = in_order(OUTWARD, place, z)
        for half in (0, 1):
            for way in (0, 1):
                y_copy(z_from, way, half).wait_send()
            relay_copy(z_from, half).wait_send()
        on_line(place, lambda copy: copy.wait_send())
    for which in (0, 1):
        for step in range(4):
            degree_copy(which, step).wait_send()


def gather_features(features, adj_tiles, slots, count):
    dma = pltpu.SemaphoreType.DMA
    slot_total = adj_tiles.shape[0]
    return pl.pallas_call(
        gather_kernel,
        in_specs=[
            pl.BlockSpec(memory_space=pltpu.SMEM),
            VMEM_SPEC,
            pl.BlockSpec(memory_space=pltpu.HBM),
            pl.BlockSpec(memory_space=pltpu.HBM),
        ],
        out_specs=[VMEM_SPEC] * 6,
        out_shape=[
            jax.ShapeDtypeStruct((slot_total, TILE, TILE), BF16),
            jax.ShapeDtypeStruct((32, TILE, 2 * TILE), BF16),
            jax.ShapeDtypeStruct((32, TILE), F32),
            jax.ShapeDtypeStruct((32, TILE), F32),
            jax.ShapeDtypeStruct((3, TILE), jnp.int32),
            jax.ShapeDtypeStruct((3, TILE), jnp.int32),
        ],
        scratch_shapes=[
            pltpu.VMEM((slot_total, TILE, TILE), jnp.int32),
            pltpu.VMEM((slot_total, TILE), F32),
            pltpu.VMEM((slot_total, TILE), F32),
            pltpu.VMEM((2, 32, TILE), F32),
            pltpu.VMEM((16, 2, TILE, TILE), F32),
            pltpu.VMEM((2, 4, 32, TILE), F32),
            pltpu.VMEM((2, 4, 32, TILE), F32),
            dma,
            dma((slot_total // CHUNK,)),
            dma((16, 2)),
            dma((4, 2, 2)),
            dma((4, 2, 2)),
            dma((4, 2)),
            dma((2, 4)),
            dma((2, 4)),
        ],
        compiler_params=pltpu.CompilerParams(vmem_limit_bytes=LIMIT, collective_id=0, has_side_effects=True),
        name="gather_features",
    )(
        count,
        slots,
        pltpu.with_memory_space_constraint(features.reshape(2, TILE, TILE), pltpu.HBM),
        pltpu.with_memory_space_constraint(adj_tiles, pltpu.HBM),
    )


WROWS = 72


def layer_kernel(
    part_ref, w_ref, b_ref, grad_ref, scale_ref, act_ref, pair_ref, wsum_ref,
    sib_got, ring_a, ring_b, from_left, from_right, z_sent, z_got, held, wgrad, w_sent, w_got,
    sib_ssem, sib_rsem, far_ssem, far_rsem, near_ssem, near_rsem, z_ssem, z_rsem,
    recv_sem, zg_sem, xg_sem, relay_sem, sg_sem, w_ssem, w_rsem,
):
    col = lax.axis_index("col")
    x, zh, core = lax.div(col, 4), lax.rem(lax.div(col, 2), 2), lax.rem(col, 2)
    x_up, x_down, x_far = lax.rem(x + 1, 4), lax.rem(x + 3, 4), lax.rem(x + 2, 4)
    sibling = col + 1 - 2 * core
    z_peer = col + 2 - 4 * zh
    up, down = x_up * 4 + zh * 2 + core, x_down * 4 + zh * 2 + core
    greet([], [sibling, z_peer, up, down, x_far * 4 + zh * 2 + core])()

    def sib_copy(place, which):
        target = (x_far, x_up, x_down, x)[place]
        half_z = 1 - zh if which == 0 else zh
        return remote(
            part_ref.at[target * 4 + half_z * 2 + 1 - core], sib_got.at[place, which],
            sib_ssem.at[place, which], sib_rsem.at[place, which], col=sibling,
        )

    def far_copy(which, way):
        return remote(
            sib_got.at[0, which, way], (ring_a, ring_b)[way].at[which],
            far_ssem.at[which, way], far_rsem.at[which, way], col=(up, down)[way],
        )

    def near_copy(which, way, half):
        return remote(
            sib_got.at[1 + way, which, half], (from_left, from_right)[way].at[which, half],
            near_ssem.at[which, way, half], near_rsem.at[which, way, half], col=(up, down)[way],
        )

    def z_copy(half):
        return remote(z_sent.at[half], z_got.at[half], z_ssem.at[half], z_rsem.at[half], col=z_peer)

    def join(place, which):
        target = (x_far, x_up, x_down, x)[place]
        half_z = 1 - zh if which == 0 else zh
        sib_copy(place, which).wait_recv()
        sib_got[place, which] += part_ref[target * 4 + half_z * 2 + core]

    for which in (0, 1):
        for place in range(4):
            sib_copy(place, which).start()
    for which in (0, 1):
        join(0, which)
        for way in (0, 1):
            far_copy(which, way).start()
        for way in (0, 1):
            join(1 + way, which)
            near_copy(which, way, 1 - way).start()
        for way in (0, 1):
            far_copy(which, way).wait_recv()
            sib_got[1 + way, which, way] += (ring_a, ring_b)[way][which]
            near_copy(which, way, way).start()
    for which in (0, 1):
        join(3, which)
        for half in (1, 0):
            for way in (0, 1):
                near_copy(which, way, half).wait_recv()
            total = sib_got[3, which, half] + from_left[which, half] + from_right[which, half]
            if which == 0:
                z_sent[half] = total
                z_copy(half).start()
            else:
                sib_got[3, which, half] = total
    for half in (0, 1):
        z_copy(half).wait_recv()

    scales, pre_grads, rows = [], [], []
    for half in (0, 1):
        scale = to_column(scale_ref[pl.ds(2 * col + half, 1), :])
        rows.append((sib_got[3, 1, half] + z_got[half]) * scale)
        scales.append(scale)
    aggregated = jnp.concatenate(rows, axis=0)
    scale = jnp.concatenate(scales, axis=0)
    preact = jnp.dot(aggregated, w_ref[...], precision=HIGHEST, preferred_element_type=F32) + b_ref[...]
    logistic = 1.0 / (1.0 + jnp.exp(-preact))
    act_ref[...] = preact * logistic
    pre_grad = grad_ref[...] * logistic * (1.0 + preact * (1.0 - logistic))
    back = lax.dot_general(pre_grad, w_ref[...], NT, precision=HIGHEST, preferred_element_type=F32) * scale
    held[col, 0] = back[:TILE]
    held[col, 1] = back[TILE:]

    def spread_z(half):
        return remote(
            held.at[col, half], held.at[col, half], zg_sem.at[half], recv_sem.at[col, half], col=z_peer
        )

    def spread_x(which, way, half):
        half_z = zh if which == 0 else 1 - zh
        block = x * 4 + half_z * 2 + core
        return remote(
            held.at[block, half], held.at[block, half], xg_sem.at[which, way, half], recv_sem.at[block, half],
            col=(up, down)[way],
        )

    def relay_x(which, half):
        half_z = zh if which == 0 else 1 - zh
        block = (x_down if half == 0 else x_up) * 4 + half_z * 2 + core
        return remote(
            held.at[block, half], held.at[block, half], relay_sem.at[which, half], recv_sem.at[block, half],
            col=(up, down)[half],
        )

    def spread_sib(place, which, half):
        target = (x, x_up, x_down, x_far)[place]
        half_z = zh if which == 0 else 1 - zh
        block = target * 4 + half_z * 2 + core
        return remote(
            held.at[block, half], held.at[block, half], sg_sem.at[place, which, half], recv_sem.at[block, half],
            col=sibling,
        )

    def arrived(block, half):
        remote(
            held.at[block, half], held.at[block, half], zg_sem.at[half], recv_sem.at[block, half], col=sibling
        ).wait_recv()

    def settle(block, half):
        pair_ref[2 * block + half] = split_pair(held[block, half])

    for half in (0, 1):
        spread_z(half).start()
    for way, half in BY_WAY:
        spread_x(0, way, half).start()
    for half in (0, 1):
        spread_sib(0, 0, half).start()

    wgrad[0:TILE, :] = lax.dot_general(aggregated, pre_grad, TN, precision=HIGHEST, preferred_element_type=F32)
    first_row = lax.broadcasted_iota(jnp.int32, (16, TILE), 0) == 0
    wgrad[TILE : TILE + 16, :] = jnp.where(first_row, jnp.sum(pre_grad, axis=0, keepdims=True), 0.0)

    def w_rows(which):
        return pl.ds(pl.multiple_of(which * WROWS, 8), WROWS)

    def w_copy(step):
        if step == 0:
            return remote(
                wgrad.at[w_rows(1 - core)], w_got.at[0], w_ssem.at[0], w_rsem.at[0], col=sibling
            )
        peer = xor_peer(col, 1 << step)
        return remote(w_sent.at[step - 1], w_got.at[step], w_ssem.at[step], w_rsem.at[step], col=peer)

    def w_step(step):
        w_copy(step).wait_recv()
        mine = wgrad[w_rows(core), :] if step == 0 else w_sent[step - 1]
        total = mine + w_got[step]
        if step < 3:
            w_sent[step] = total
            w_copy(step + 1).start()
        else:
            wsum_ref[...] = total

    def relay(which):
        half_z = zh if which == 0 else 1 - zh
        for half in (0, 1):
            side = x_down if half == 0 else x_up
            arrived(side * 4 + half_z * 2 + core, half)
            relay_x(which, half).start()
            spread_sib((2, 1)[half], which, half).start()

    def near_rest(which):
        half_z = zh if which == 0 else 1 - zh
        for half in (0, 1):
            side = x_up if half == 0 else x_down
            arrived(side * 4 + half_z * 2 + core, half)
            spread_sib((1, 2)[half], which, half).start()

    def far_rest(which):
        half_z = zh if which == 0 else 1 - zh
        for half in (0, 1):
            arrived(x_far * 4 + half_z * 2 + core, half)
            spread_sib(3, which, half).start()

    w_copy(0).start()
    relay(0)
    near_rest(0)
    w_step(0)
    other = x * 4 + (1 - zh) * 2 + core
    for half in (0, 1):
        arrived(other, half)
        for way in (0, 1):
            spread_x(1, way, half).start()
        spread_sib(0, 1, half).start()
    far_rest(0)
    w_step(1)
    for side in (x, x_up, x_down, x_far):
        for half in (0, 1):
            settle(side * 4 + zh * 2 + core, half)
    relay(1)
    near_rest(1)
    w_step(2)
    for side in (x, x_up, x_down, x_far):
        for half in (0, 1):
            block = side * 4 + zh * 2 + 1 - core
            arrived(block, half)
            settle(block, half)
    far_rest(1)
    w_step(3)
    for side in (x, x_up, x_down, x_far):
        for half in (0, 1):
            settle(side * 4 + (1 - zh) * 2 + core, half)
    for side in (x, x_up, x_down, x_far):
        for half in (0, 1):
            block = side * 4 + (1 - zh) * 2 + 1 - core
            arrived(block, half)
            settle(block, half)

    for which in (0, 1):
        for place in range(4):
            sib_copy(place, which).wait_send()
            for half in (0, 1):
                spread_sib(place, which, half).wait_send()
        for way in (0, 1):
            far_copy(which, way).wait_send()
            relay_x(which, way).wait_send()
            for half in (0, 1):
                near_copy(which, way, half).wait_send()
                spread_x(which, way, half).wait_send()
    for half in (0, 1):
        z_copy(half).wait_send()
        spread_z(half).wait_send()
    for step in range(4):
        w_copy(step).wait_send()


def dense_layer(part, weight, bias_vector, out_grad, dst_scale):
    dma = pltpu.SemaphoreType.DMA
    half = (TILE, TILE)
    return pl.pallas_call(
        layer_kernel,
        in_specs=[VMEM_SPEC] * 5,
        out_specs=[VMEM_SPEC] * 3,
        out_shape=[
            jax.ShapeDtypeStruct((2 * TILE, TILE), F32),
            jax.ShapeDtypeStruct((32, TILE, 2 * TILE), BF16),
            jax.ShapeDtypeStruct((WROWS, TILE), F32),
        ],
        scratch_shapes=[
            pltpu.VMEM((4, 2, 2) + half, F32),
            pltpu.VMEM((2,) + half, F32),
            pltpu.VMEM((2,) + half, F32),
            pltpu.VMEM((2, 2) + half, F32),
            pltpu.VMEM((2, 2) + half, F32),
            pltpu.VMEM((2,) + half, F32),
            pltpu.VMEM((2,) + half, F32),
            pltpu.VMEM((16, 2) + half, F32),
            pltpu.VMEM((2 * WROWS, TILE), F32),
            pltpu.VMEM((3, WROWS, TILE), F32),
            pltpu.VMEM((4, WROWS, TILE), F32),
            dma((4, 2)), dma((4, 2)), dma((2, 2)), dma((2, 2)), dma((2, 2, 2)), dma((2, 2, 2)), dma((2,)), dma((2,)),
            dma((16, 2)), dma((2,)), dma((2, 2, 2)), dma((2, 2)), dma((4, 2, 2)), dma((4,)), dma((4,)),
        ],
        compiler_params=pltpu.CompilerParams(vmem_limit_bytes=LIMIT, collective_id=1, has_side_effects=True),
        name="dense_layer",
    )(part.reshape((16, 2) + half), weight, bias_vector.reshape(1, TILE), out_grad, dst_scale)


def scatter_kernel(
    part_ref, wsum_ref, scale_ref, grad_ref, wgrad_ref, bgrad_ref,
    staged_a, staged_b, ring_a, ring_b, from_down, from_up, total, line_up, line_down, w_sent, w_got, w_all, w_full,
    far_ssem, far_rsem, near_ssem, near_rsem, line_ssem, line_rsem, w_ssem, w_rsem,
):
    row, col = lax.axis_index("row"), lax.axis_index("col")
    y, z = lax.div(row, 4), lax.rem(row, 4)
    core = lax.rem(col, 2)
    y_up, y_down, y_far = lax.rem(y + 1, 4), lax.rem(y + 3, 4), lax.rem(y + 2, 4)
    sibling = col + 1 - 2 * core
    greet(
        [lax.rem(y + d, 4) * 4 + z for d in (1, 2, 3)] + [y * 4 + lax.rem(z + d, 4) for d in (1, 2, 3)],
        [sibling],
    )()
    up, down = y_up * 4 + z, y_down * 4 + z

    def far_copy(zb, way):
        return remote(
            part_ref.at[y_far * 4 + zb, way], (ring_a, ring_b)[way].at[zb],
            far_ssem.at[zb, way], far_rsem.at[zb, way], row=(up, down)[way],
        )

    def near_copy(zb, way, half):
        block = (y_up, y_down)[way] * 4 + zb
        source = (staged_a, staged_b)[way].at[zb] if half == way else part_ref.at[block, half]
        return remote(
            source, (from_down, from_up)[way].at[zb, half],
            near_ssem.at[zb, way, half], near_rsem.at[zb, way, half], row=(up, down)[way],
        )

    def line_copy(zb, way, half):
        return remote(
            total.at[zb, half], (line_up, line_down)[way].at[zb, half],
            line_ssem.at[zb, half], line_rsem.at[zb, way, half], row=y * 4 + lax.rem(z + (1 if way == 0 else 3), 4),
        )

    def w_copy(step):
        if step == 4:
            return remote(w_sent.at[3], w_all, w_ssem.at[4], w_rsem.at[4], col=sibling)
        source = wsum_ref if step == 0 else w_sent.at[step - 1]
        return remote(source, w_got.at[step], w_ssem.at[step], w_rsem.at[step], row=xor_peer(row, 1 << step))

    def w_step(step):
        w_copy(step).wait_recv()
        source = wsum_ref if step == 0 else w_sent.at[step - 1]
        w_sent[step] = source[...] + w_got[step]
        w_copy(step + 1).start()

    zbs = [in_order(INWARD, place, z) for place in range(4)]

    def far_step(place):
        for way in (0, 1):
            far_copy(zbs[place], way).start()

    def near_step(place):
        for way in (0, 1):
            near_copy(zbs[place], way, 1 - way).start()

    def relay_step(place):
        zb = zbs[place]
        for way in (0, 1):
            far_copy(zb, way).wait_recv()
            block = (y_up, y_down)[way] * 4 + zb
            (staged_a, staged_b)[way][zb] = part_ref[block, way] + (ring_a, ring_b)[way][zb]
            near_copy(zb, way, way).start()

    def line_ways(place):
        zb = zbs[place]
        if place == 3:
            return ((0, z > 0, None), (1, z < 3, None))
        return ((0, (zb > z) & (z > 0), zb > z), (1, (zb < z) & (z < 3), zb < z))

    def close_step(place):
        zb = zbs[place]
        for half in (1, 0):
            for way in (0, 1):
                near_copy(zb, way, half).wait_recv()
            total[zb, half] = part_ref[y * 4 + zb, half] + from_down[zb, half] + from_up[zb, half]
        for way, comes, goes in line_ways(place):
            for half in (1, 0):

                @pl.when(comes)
                def _():
                    line_copy(zb, way, half).wait_recv()
                    total[zb, half] += (line_up, line_down)[way][zb, half]

                if goes is not None:
                    pl.when(goes)(lambda: line_copy(zb, way, half).start())

    def send_step(place):
        zb = zbs[place]
        for way in (0, 1):
            far_copy(zb, way).wait_send()
            for half in (0, 1):
                near_copy(zb, way, half).wait_send()
        for way, _, goes in line_ways(place):
            for half in (0, 1):
                if goes is not None:
                    pl.when(goes)(lambda: line_copy(zb, way, half).wait_send())

    far_step(0)
    near_step(0)
    far_step(1)
    w_copy(0).start()
    relay_step(0)
    near_step(1)
    far_step(2)
    relay_step(1)
    near_step(2)
    far_step(3)
    close_step(0)
    relay_step(2)
    near_step(3)
    w_step(0)
    close_step(1)
    relay_step(3)
    w_step(1)
    close_step(2)
    w_step(2)
    w_step(3)
    close_step(3)

    for half in (0, 1):
        scale = to_column(scale_ref[pl.ds(2 * row + half, 1), :])
        grad_ref[pl.ds(half * TILE, TILE), :] = total[z, half] * scale
    w_copy(4).wait_recv()
    w_full[pl.ds(pl.multiple_of(core * WROWS, 8), WROWS), :] = w_sent[3]
    w_full[pl.ds(pl.multiple_of((1 - core) * WROWS, 8), WROWS), :] = w_all[...]
    wgrad_ref[...] = w_full[0:TILE, :]
    bgrad_ref[...] = w_full[TILE : TILE + 1, :]
    for place in range(4):
        send_step(place)
    for step in range(5):
        w_copy(step).wait_send()


def scatter_gradients(part, wsum, src_scale):
    dma = pltpu.SemaphoreType.DMA
    half = (TILE, TILE)
    return pl.pallas_call(
        scatter_kernel,
        in_specs=[VMEM_SPEC] * 3,
        out_specs=[VMEM_SPEC] * 3,
        out_shape=[
            jax.ShapeDtypeStruct((2 * TILE, TILE), F32),
            jax.ShapeDtypeStruct((TILE, TILE), F32),
            jax.ShapeDtypeStruct((1, TILE), F32),
        ],
        scratch_shapes=[
            pltpu.VMEM((4,) + half, F32),
            pltpu.VMEM((4,) + half, F32),
            pltpu.VMEM((4,) + half, F32),
            pltpu.VMEM((4,) + half, F32),
            pltpu.VMEM((4, 2) + half, F32),
            pltpu.VMEM((4, 2) + half, F32),
            pltpu.VMEM((4, 2) + half, F32),
            pltpu.VMEM((4, 2) + half, F32),
            pltpu.VMEM((4, 2) + half, F32),
            pltpu.VMEM((4, WROWS, TILE), F32),
            pltpu.VMEM((4, WROWS, TILE), F32),
            pltpu.VMEM((WROWS, TILE), F32),
            pltpu.VMEM((2 * WROWS, TILE), F32),
            dma((4, 2)), dma((4, 2)), dma((4, 2, 2)), dma((4, 2, 2)), dma((4, 2)), dma((4, 2, 2)), dma((5,)), dma((5,)),
        ],
        compiler_params=pltpu.CompilerParams(vmem_limit_bytes=LIMIT, collective_id=2, has_side_effects=True),
        name="scatter_gradients",
    )(part.reshape((16, 2) + half), wsum, src_scale)


def local(features, weight, bias_vector, out_grad, adj_tiles, tile_slots, tile_counts):
    tiles, pairs, src_scale, dst_scale, forward_info, backward_info = gather_features(
        features, adj_tiles[0, 0], tile_slots[0], tile_counts
    )
    part = sparse_product(NN, tile_counts, forward_info, tiles, pairs, "forward_product")
    activated, grad_pairs, wsum = dense_layer(part, weight, bias_vector, out_grad, dst_scale)
    back = sparse_product(TN, tile_counts, backward_info, tiles, grad_pairs, "backward_product")
    feature_grad, weight_grad, bias_grad = scatter_gradients(back, wsum, src_scale)
    return activated, feature_grad, weight_grad, bias_grad.reshape(TILE)


def solution(mesh):
    return jax.shard_map(
        local,
        mesh=mesh,
        in_specs=(
            P(("col", "row"), None),
            P(),
            P(),
            P(("row", "col"), None),
            P("row", "col", None, None, None),
            P("row", "col", None),
            P("row", "col"),
        ),
        out_specs=(P(("row", "col"), None), P(("col", "row"), None), P(), P()),
        check_vma=False,
    )
```

```python
import functools

import jax
import jax.numpy as jnp
from jax import lax
from jax.experimental import pallas as pl
from jax.experimental.pallas import tpu as pltpu
from jax.sharding import PartitionSpec as P

TILE = 128
MESH = pl.DeviceIdType.MESH
F32 = jnp.float32
BF16 = jnp.bfloat16
HIGHEST = lax.Precision.HIGHEST
VMEM_SPEC = pl.BlockSpec(memory_space=pltpu.VMEM)
CHUNK = 8
LIMIT = 24 << 20
GATHER_PIECES = 2
LAYER_PIECES = 2
SCATTER_PIECES = 2


def block_of(pieces):
    return (pieces, 2 * TILE // pieces, TILE)


def by_way(pieces):
    return [(piece % 2, piece) for piece in range(pieces)] + [(piece % 2, piece + 1 - 2 * (piece % 2)) for piece in range(pieces)]


def piece_columns(scale_ref, first, pieces):
    columns = [to_column(scale_ref[pl.ds(first + half, 1), :]) for half in (0, 1)]
    each = pieces // 2
    rows = TILE // each
    return [columns[k // each][k % each * rows : (k % each + 1) * rows] for k in range(pieces)]
NT = (((1,), (1,)), ((), ()))
NN = (((1,), (0,)), ((), ()))
TN = (((0,), (0,)), ((), ()))


def remote(src, dst, send_sem, recv_sem, **where):
    return pltpu.make_async_remote_copy(
        src_ref=src,
        dst_ref=dst,
        send_sem=send_sem,
        recv_sem=recv_sem,
        device_id=where,
        device_id_type=MESH,
    )


def xor_peer(index, bit):
    return index + bit - 2 * bit * lax.rem(lax.div(index, bit), 2)


def greet(rows, cols):
    barrier = pltpu.get_barrier_semaphore()
    for peer in rows:
        pl.semaphore_signal(barrier, inc=1, device_id={"row": peer}, device_id_type=MESH)
    for peer in cols:
        pl.semaphore_signal(barrier, inc=1, device_id={"col": peer}, device_id_type=MESH)
    return lambda: pl.semaphore_wait(barrier, len(rows) + len(cols))


def to_column(row_vector):
    spread = jnp.broadcast_to(row_vector, (TILE, TILE))
    diagonal = lax.broadcasted_iota(jnp.int32, (TILE, TILE), 0) == lax.broadcasted_iota(
        jnp.int32, (TILE, TILE), 1
    )
    return jnp.sum(jnp.where(diagonal, spread, 0.0), axis=1, keepdims=True)


def split_pair(value):
    high = value.astype(BF16)
    low = (value - high.astype(F32)).astype(BF16)
    return jnp.concatenate([high, low], axis=1)


def put_pair(pair_ref, block, piece, pieces, value):
    each = pieces // 2
    rows = TILE // each
    here = slice(piece % each * rows, (piece % each + 1) * rows)
    pair_ref[2 * block + piece // each, here, :] = split_pair(value)


def sort_table(slots, live, by_row):
    tile_row = jnp.floor(slots * (1.0 / 32.0))
    tile_col = slots - 32.0 * tile_row
    lane = lax.broadcasted_iota(jnp.int32, (1, TILE), 1).astype(F32)
    key = jnp.where(live, tile_row * 32.0 + tile_col if by_row else tile_col * 32.0 + tile_row, 2048.0 + lane)
    key_column = to_column(key)
    rank = jnp.sum(jnp.where(key < key_column, 1.0, 0.0), axis=1, keepdims=True)
    place = rank == lax.broadcasted_iota(jnp.int32, (TILE, TILE), 1).astype(F32)
    number = lax.broadcasted_iota(jnp.int32, (TILE, 1), 0).astype(F32)

    def moved(column):
        return jnp.sum(jnp.where(place, column, 0.0), axis=0, keepdims=True).astype(jnp.int32)

    ends = (to_column(tile_row), to_column(tile_col))
    if not by_row:
        ends = ends[::-1]
    live_column = to_column(jnp.where(live, 1.0, 0.0))
    target = lax.broadcasted_iota(jnp.int32, (TILE, TILE), 1).astype(F32)

    def counted(which):
        return jnp.sum(jnp.where(which, live_column, 0.0), axis=0, keepdims=True).astype(jnp.int32)

    return moved(number), moved(ends[0]), moved(ends[1]), counted(ends[0] < target), counted(ends[0] <= target)


def block_product(dims, count_ref, info_ref, tiles_ref, pair_ref, sums_ref, first, last, total):
    unroll = 8
    count = count_ref[0, 0]

    def body(step, total):
        for u in range(unroll):
            k = step * unroll + u
            at = jnp.clip(count - 1, 0, k)
            number = jnp.clip(info_ref[0, at], 0, tiles_ref.shape[0] - 1)
            source = jnp.clip(info_ref[2, at], 0, pair_ref.shape[0] - 1)
            both = lax.dot_general(tiles_ref[number], pair_ref[source], dims, preferred_element_type=F32)
            goes_on = (k > 0) & (info_ref[1, jnp.maximum(at - 1, 0)] == info_ref[1, at])
            total = both[:, :TILE] + both[:, TILE:] + jnp.where(goes_on, total, 0.0)
            sums_ref[k] = total
        return total

    return lax.fori_loop(first, last, body, total)


def take_block(info_ref, sums_ref, part_ref, block):
    rows = part_ref.shape[2]
    each = TILE // rows
    for half in (0, 1):
        first, end = info_ref[3, 2 * block + half], info_ref[4, 2 * block + half]
        tile = jnp.where(end > first, sums_ref[jnp.clip(end - 1, 0, sums_ref.shape[0] - 1)], 0.0)
        for k in range(each):
            part_ref[block, half * each + k] = tile[k * rows : (k + 1) * rows]


def split_rows(value, order):
    high = value.astype(BF16)
    low = (value - high.astype(F32)).astype(BF16)
    return jnp.concatenate([(high, low)[k] for k in order], axis=0)


def split_columns(value):
    high = value.astype(BF16)
    low = (value - high.astype(F32)).astype(BF16)
    return jnp.concatenate([high, low, high], axis=1)


OUTWARD = ((0, 1, 2, 3), (1, 0, 2, 3), (2, 1, 3, 0), (3, 2, 1, 0))
INWARD = tuple(order[::-1] for order in OUTWARD)


def in_order(orders, place, z):
    low, high = lax.rem(z, 2), lax.div(z, 2)
    v = [orders[k][place] for k in range(4)]
    return v[0] + (v[1] - v[0]) * low + (v[2] - v[0]) * high + (v[3] - v[2] - v[1] + v[0]) * low * high


def gather_kernel(
    count_ref, slots_ref, feat_ref, adj_ref,
    tiles_ref, pair_ref, src_scale_ref, dst_scale_ref, forward_info_ref, backward_info_ref,
    adj_got, row_sums, col_sums, parts, held, slots_got, deg_sent, deg_got,
    feat_sem, adj_sem, recv_sem, z_sem, y_sem, relay_sem, deg_send_sem, deg_recv_sem,
):
    chunks = adj_ref.shape[0] // CHUNK
    row, col = lax.axis_index("row"), lax.axis_index("col")
    y, z = lax.div(row, 4), lax.rem(row, 4)
    y_up, y_down, y_far = lax.rem(y + 1, 4), lax.rem(y + 3, 4), lax.rem(y + 2, 4)
    wait_for_all = greet(
        [lax.rem(y + d, 4) * 4 + z for d in (1, 2, 3)] + [y * 4 + lax.rem(z + d, 4) for d in (1, 2, 3)],
        [xor_peer(col, bit) for bit in (1, 2, 4, 8)],
    )

    def adj_copy(chunk):
        here = pl.ds(pl.multiple_of(chunk * CHUNK, CHUNK), CHUNK)
        return pltpu.make_async_copy(adj_ref.at[here], adj_got.at[here], adj_sem.at[chunk])

    feat_copy = pltpu.make_async_copy(feat_ref, held.at[row], feat_sem.at[0])
    feat_copy.start()
    slots_copy = pltpu.make_async_copy(slots_ref, slots_got, feat_sem.at[1])
    slots_copy.start()
    for chunk in range(chunks):
        adj_copy(chunk).start()

    ones = jnp.ones((TILE, TILE), F32).astype(BF16)
    diagonal = lax.broadcasted_iota(jnp.int32, (TILE, TILE), 0) == lax.broadcasted_iota(
        jnp.int32, (TILE, TILE), 1
    )

    def degree_chunks(first, last):
        def body(chunk, carry):
            adj_copy(chunk).wait()
            for k in range(CHUNK):
                slot = chunk * CHUNK + k
                tile = adj_got[slot].astype(F32)
                narrow = tile.astype(BF16)
                tiles_ref[slot] = narrow
                col_sums[pl.ds(slot, 1), :] = jnp.sum(tile, axis=0, keepdims=True)
                sums = jnp.dot(narrow, ones, preferred_element_type=F32)
                row_sums[pl.ds(slot, 1), :] = jnp.sum(jnp.where(diagonal, sums, 0.0), axis=0, keepdims=True)
            return carry

        lax.fori_loop(first, last, body, 0)

    slots_copy.wait()
    slots = slots_got[...].astype(F32)
    live = lax.broadcasted_iota(jnp.int32, (1, TILE), 1) < count_ref[0, 0]

    def degree_parts():
        tile_row = jnp.floor(slots * (1.0 / 32.0))
        tile_col = slots - 32.0 * tile_row
        tile_number = lax.broadcasted_iota(jnp.int32, (32, TILE), 0).astype(F32)
        row_select = jnp.where(live & (tile_row == tile_number), 1.0, 0.0).astype(BF16)
        col_select = jnp.where(live & (tile_col == tile_number), 1.0, 0.0).astype(BF16)
        parts[0] = jnp.dot(col_select, col_sums[...].astype(BF16), preferred_element_type=F32)
        parts[1] = jnp.dot(row_select, row_sums[...].astype(BF16), preferred_element_type=F32)

    def z_copy(z_from, way, piece):
        block = y * 4 + z_from
        return remote(
            held.at[block, piece], held.at[block, piece],
            z_sem.at[z_from, way, piece], recv_sem.at[block, piece],
            row=y * 4 + lax.rem(z + (1 if way == 0 else 3), 4),
        )

    def y_copy(z_from, way, piece):
        block = y * 4 + z_from
        return remote(
            held.at[block, piece], held.at[block, piece],
            y_sem.at[z_from, way, piece], recv_sem.at[block, piece],
            row=(y_up, y_down)[way] * 4 + z,
        )

    def relay_copy(z_from, piece):
        way = piece % 2
        block = (y_down, y_up)[way] * 4 + z_from
        return remote(
            held.at[block, piece], held.at[block, piece],
            relay_sem.at[z_from, piece], recv_sem.at[block, piece],
            row=(y_up, y_down)[way] * 4 + z,
        )

    def arrived(block, piece):
        remote(
            held.at[block, piece], held.at[block, piece], relay_sem.at[0, piece], recv_sem.at[block, piece],
            row=y_up * 4 + z,
        ).wait_recv()

    def on_line(place, pieces, action):
        z_from = in_order(OUTWARD, place, z)
        for way in (0, 1):
            goes = z < 3 if way == 0 else z > 0
            if place:
                goes = goes & (z_from < z if way == 0 else z_from > z)

            @pl.when(goes)
            def _():
                for piece in pieces:
                    action(z_copy(z_from, way, piece))

    def column_step(place):
        z_from = in_order(OUTWARD, place, z)
        if place:
            for piece in range(GATHER_PIECES):
                arrived(y * 4 + z_from, piece)
        on_line(place, range(GATHER_PIECES), lambda copy: copy.start())
        for way, piece in by_way(GATHER_PIECES):
            y_copy(z_from, way, piece).start()

    def relay_step(place):
        z_from = in_order(OUTWARD, place, z)
        for piece in range(GATHER_PIECES):
            arrived((y_down, y_up)[piece % 2] * 4 + z_from, piece)
            relay_copy(z_from, piece).start()

    def degree_source(which, step):
        return parts.at[which] if step == 0 else deg_sent.at[which, step - 1]

    def degree_copy(which, step):
        where = {("row", "col")[which]: xor_peer((row, col)[which], 1 << step)}
        return remote(
            degree_source(which, step), deg_got.at[which, step],
            deg_send_sem.at[which, step], deg_recv_sem.at[which, step], **where
        )

    def degree_step(step):
        for which in (0, 1):
            degree_copy(which, step).wait_recv()
            deg_sent[which, step] = degree_source(which, step)[...] + deg_got[which, step]
            if step < 3:
                degree_copy(which, step + 1).start()

    degree_chunks(0, chunks // 4)
    feat_copy.wait()
    wait_for_all()
    column_step(0)
    degree_chunks(chunks // 4, chunks // 2 + 2)
    relay_step(0)
    column_step(1)
    degree_chunks(chunks // 2 + 2, chunks)
    degree_parts()
    for which in (0, 1):
        degree_copy(which, 0).start()
    relay_step(1)
    column_step(2)
    degree_step(0)
    relay_step(2)
    degree_step(1)
    column_step(3)
    degree_step(2)
    for info_ref, by_row in ((forward_info_ref, True), (backward_info_ref, False)):
        for place, line in enumerate(sort_table(slots, live, by_row)):
            info_ref[place : place + 1, :] = line
    relay_step(3)
    degree_step(3)

    src_scale_ref[...] = lax.rsqrt(1.0 + deg_sent[0, 3])
    dst_scale_ref[...] = lax.rsqrt(1.0 + deg_sent[1, 3])

    def settle(block):
        for piece, scale in enumerate(piece_columns(src_scale_ref, 2 * block, GATHER_PIECES)):
            put_pair(pair_ref, block, piece, GATHER_PIECES, held[block, piece] * scale)

    for place in range(4):
        settle(y * 4 + in_order(OUTWARD, place, z))
    for place in range(4):
        z_from = in_order(OUTWARD, place, z)
        for way in (0, 1):
            block = (y_down, y_up)[way] * 4 + z_from
            for piece in range(1 - way, GATHER_PIECES, 2):
                arrived(block, piece)
            settle(block)
    for place in range(4):
        z_from = in_order(OUTWARD, place, z)
        for piece in range(GATHER_PIECES):
            arrived(y_far * 4 + z_from, piece)
        settle(y_far * 4 + z_from)
    for place in range(4):
        z_from = in_order(OUTWARD, place, z)
        for piece in range(GATHER_PIECES):
            for way in (0, 1):
                y_copy(z_from, way, piece).wait_send()
            relay_copy(z_from, piece).wait_send()
        on_line(place, range(GATHER_PIECES), lambda copy: copy.wait_send())
    for which in (0, 1):
        for step in range(4):
            degree_copy(which, step).wait_send()


def gather_features(features, adj_tiles, slots, count):
    dma = pltpu.SemaphoreType.DMA
    slot_total = adj_tiles.shape[0]
    return pl.pallas_call(
        gather_kernel,
        in_specs=[
            pl.BlockSpec(memory_space=pltpu.SMEM),
            pl.BlockSpec(memory_space=pltpu.HBM),
            pl.BlockSpec(memory_space=pltpu.HBM),
            pl.BlockSpec(memory_space=pltpu.HBM),
        ],
        out_specs=[VMEM_SPEC] * 6,
        out_shape=[
            jax.ShapeDtypeStruct((slot_total, TILE, TILE), BF16),
            jax.ShapeDtypeStruct((32, TILE, 2 * TILE), BF16),
            jax.ShapeDtypeStruct((32, TILE), F32),
            jax.ShapeDtypeStruct((32, TILE), F32),
            jax.ShapeDtypeStruct((5, TILE), jnp.int32),
            jax.ShapeDtypeStruct((5, TILE), jnp.int32),
        ],
        scratch_shapes=[
            pltpu.VMEM((slot_total, TILE, TILE), jnp.int32),
            pltpu.VMEM((slot_total, TILE), F32),
            pltpu.VMEM((slot_total, TILE), F32),
            pltpu.VMEM((2, 32, TILE), F32),
            pltpu.VMEM((16,) + block_of(GATHER_PIECES), F32),
            pltpu.VMEM((1, TILE), jnp.int32),
            pltpu.VMEM((2, 4, 32, TILE), F32),
            pltpu.VMEM((2, 4, 32, TILE), F32),
            dma((2,)),
            dma((slot_total // CHUNK,)),
            dma((16, GATHER_PIECES)),
            dma((4, 2, GATHER_PIECES)),
            dma((4, 2, GATHER_PIECES)),
            dma((4, GATHER_PIECES)),
            dma((2, 4)),
            dma((2, 4)),
        ],
        compiler_params=pltpu.CompilerParams(vmem_limit_bytes=LIMIT, collective_id=0, has_side_effects=True),
        name="gather_features",
    )(
        count,
        pltpu.with_memory_space_constraint(slots, pltpu.HBM),
        pltpu.with_memory_space_constraint(features.reshape(block_of(GATHER_PIECES)), pltpu.HBM),
        pltpu.with_memory_space_constraint(adj_tiles, pltpu.HBM),
    )


SLICE = (16, TILE)


def layer_kernel(
    count_ref, info_ref, tiles_ref, source_ref, w_ref, b_ref, grad_ref, scale_ref, act_ref, pair_ref, wsum_ref,
    sums, part_ref, w_fore, w_back, sib_got, ring, from_left, from_right, z_sent, z_got, held, aggs, grads, wgrad, w_got,
    sib_ssem, sib_rsem, far_ssem, far_rsem, near_ssem, near_rsem, z_ssem, z_rsem,
    recv_sem, zg_sem, xg_sem, relay_sem, sg_sem, w_ssem, w_rsem,
):
    col = lax.axis_index("col")
    x, zh, core = lax.div(col, 4), lax.rem(lax.div(col, 2), 2), lax.rem(col, 2)
    x_up, x_down, x_far = lax.rem(x + 1, 4), lax.rem(x + 3, 4), lax.rem(x + 2, 4)
    sibling = col + 1 - 2 * core
    z_peer = col + 2 - 4 * zh
    up, down = x_up * 4 + zh * 2 + core, x_down * 4 + zh * 2 + core
    wait_for_all = greet([], [lax.rem(col + d, 16) for d in range(1, 16)])
    block_product(
        NN, count_ref, info_ref, tiles_ref, source_ref, sums, 0, tiles_ref.shape[0] // 8, jnp.zeros((TILE, TILE), F32)
    )
    w_fore[...] = split_rows(w_ref[...], (0, 0, 1))
    w_back[...] = split_rows(jnp.transpose(w_ref[...]), (0, 0, 1))
    first, rest = (0, 1), range(2, LAYER_PIECES)
    after = [(piece % 2, piece + 1 - 2 * (piece % 2)) for piece in rest]

    def sib_copy(place, which):
        target = (x_far, x_up, x_down, x)[place]
        half_z = 1 - zh if which == 0 else zh
        return remote(
            part_ref.at[target * 4 + half_z * 2 + 1 - core], sib_got.at[place, which],
            sib_ssem.at[place, which], sib_rsem.at[place, which], col=sibling,
        )

    def far_copy(which, piece):
        return remote(
            sib_got.at[0, which, piece], ring.at[which, piece],
            far_ssem.at[which, piece], far_rsem.at[which, piece], col=(up, down)[piece % 2],
        )

    def near_copy(which, way, piece):
        return remote(
            sib_got.at[1 + way, which, piece], (from_left, from_right)[way].at[which, piece],
            near_ssem.at[which, way, piece], near_rsem.at[which, way, piece], col=(up, down)[way],
        )

    def z_copy(piece):
        return remote(z_sent.at[piece], z_got.at[piece], z_ssem.at[piece], z_rsem.at[piece], col=z_peer)

    def join(place, which):
        target = (x_far, x_up, x_down, x)[place]
        half_z = 1 - zh if which == 0 else zh
        sib_copy(place, which).wait_recv()
        sib_got[place, which] += part_ref[target * 4 + half_z * 2 + core]

    def open_ring(which):
        join(0, which)
        for piece in range(LAYER_PIECES):
            far_copy(which, piece).start()
        for way in (0, 1):
            join(1 + way, which)
            near_copy(which, way, 1 - way).start()
        join(3, which)

    def relay_ring(which, pieces):
        for piece in pieces:
            way = piece % 2
            far_copy(which, piece).wait_recv()
            sib_got[1 + way, which, piece] += ring[which, piece]
            near_copy(which, way, piece).start()

    def rest_ring(which):
        for way, piece in after:
            near_copy(which, way, piece).start()

    def ring_total(which, piece):
        for way in (0, 1):
            near_copy(which, way, piece).wait_recv()
        return sib_got[3, which, piece] + from_left[which, piece] + from_right[which, piece]

    def send_over(pieces):
        for piece in pieces:
            z_sent[piece] = ring_total(0, piece)
            z_copy(piece).start()

    wait_for_all()
    for which in (0, 1):
        for place in range(4):
            target = (x_far, x_up, x_down, x)[place] * 4 + (1 - zh if which == 0 else zh) * 2
            take_block(info_ref, sums, part_ref, target + 1 - core)
            sib_copy(place, which).start()
            take_block(info_ref, sums, part_ref, target + core)
    open_ring(0)
    relay_ring(0, first)
    rest_ring(0)
    relay_ring(0, rest)
    open_ring(1)
    send_over(first)
    relay_ring(1, first)
    rest_ring(1)
    send_over(rest)
    relay_ring(1, rest)

    def spread_z(piece):
        return remote(
            held.at[col, piece], held.at[col, piece], zg_sem.at[piece], recv_sem.at[col, piece], col=z_peer
        )

    def spread_x(which, way, piece):
        half_z = zh if which == 0 else 1 - zh
        block = x * 4 + half_z * 2 + core
        return remote(
            held.at[block, piece], held.at[block, piece], xg_sem.at[which, way, piece], recv_sem.at[block, piece],
            col=(up, down)[way],
        )

    def relay_x(which, piece):
        half_z = zh if which == 0 else 1 - zh
        way = piece % 2
        block = (x_down, x_up)[way] * 4 + half_z * 2 + core
        return remote(
            held.at[block, piece], held.at[block, piece], relay_sem.at[which, piece], recv_sem.at[block, piece],
            col=(up, down)[way],
        )

    def spread_sib(place, which, piece):
        target = (x, x_up, x_down, x_far)[place]
        half_z = zh if which == 0 else 1 - zh
        block = target * 4 + half_z * 2 + core
        return remote(
            held.at[block, piece], held.at[block, piece], sg_sem.at[place, which, piece], recv_sem.at[block, piece],
            col=sibling,
        )

    def arrived(block, piece):
        remote(
            held.at[block, piece], held.at[block, piece], zg_sem.at[piece], recv_sem.at[block, piece], col=sibling
        ).wait_recv()

    def spread(which, piece):
        way = piece % 2
        spread_x(which, way, piece).start()
        spread_x(which, 1 - way, piece).start()
        spread_sib(0, which, piece).start()

    def settle(block, piece):
        put_pair(pair_ref, block, piece, LAYER_PIECES, held[block, piece])

    for piece, scale in enumerate(piece_columns(scale_ref, 2 * col, LAYER_PIECES)):
        here = slice(piece * part_ref.shape[2], (piece + 1) * part_ref.shape[2])
        own = ring_total(1, piece)
        z_copy(piece).wait_recv()
        aggregated = (own + z_got[piece]) * scale
        preact = jnp.dot(split_columns(aggregated), w_fore[...], preferred_element_type=F32) + b_ref[...]
        logistic = 1.0 / (1.0 + jnp.exp(-preact))
        pre_grad = grad_ref[here, :] * logistic * (1.0 + preact * (1.0 - logistic))
        held[col, piece] = scale * jnp.dot(split_columns(pre_grad), w_back[...], preferred_element_type=F32)
        spread_z(piece).start()
        spread(0, piece)
        act_ref[here, :] = preact * logistic
        aggs[here, :] = aggregated
        grads[here, :] = pre_grad

    weight_part = lax.dot_general(
        split_rows(aggs[...], (0, 1, 0)), split_rows(grads[...], (0, 0, 1)), TN, preferred_element_type=F32
    )
    bias_part = jnp.broadcast_to(jnp.sum(grads[...], axis=0, keepdims=True), (8, TILE))
    for part in range(16):
        wgrad[part, 0:8, :] = weight_part[part * 8 : part * 8 + 8]
        wgrad[part, 8:16, :] = bias_part

    def w_copy(distance):
        peer = lax.rem(col + distance, 16)
        return remote(
            wgrad.at[peer], w_got.at[distance - 1], w_ssem.at[distance - 1], w_rsem.at[distance - 1], col=peer
        )

    for distance in range(1, 16):
        w_copy(distance).start()

    def relay(which, pieces):
        half_z = zh if which == 0 else 1 - zh
        for piece in pieces:
            way = piece % 2
            arrived((x_down, x_up)[way] * 4 + half_z * 2 + core, piece)
            relay_x(which, piece).start()
            spread_sib((2, 1)[way], which, piece).start()

    def near_rest(which):
        half_z = zh if which == 0 else 1 - zh
        for piece in range(LAYER_PIECES):
            way = piece % 2
            arrived((x_up, x_down)[way] * 4 + half_z * 2 + core, piece)
            spread_sib((1, 2)[way], which, piece).start()

    def far_rest(which):
        half_z = zh if which == 0 else 1 - zh
        for piece in range(LAYER_PIECES):
            arrived(x_far * 4 + half_z * 2 + core, piece)
            spread_sib(3, which, piece).start()

    other = x * 4 + (1 - zh) * 2 + core

    def take_over(piece):
        arrived(other, piece)
        spread(1, piece)

    relay(0, range(LAYER_PIECES))
    near_rest(0)
    for piece in range(LAYER_PIECES):
        take_over(piece)
        if piece == 1:
            far_rest(0)
        if piece >= 2:
            relay(1, (piece - 2,))
    for piece in range(max(LAYER_PIECES - 2, 0), LAYER_PIECES - 1):
        relay(1, (piece,))
    for side in (x, x_up):
        for piece in range(LAYER_PIECES):
            settle(side * 4 + zh * 2 + core, piece)
    relay(1, (LAYER_PIECES - 1,))
    for side in (x_down, x_far):
        for piece in range(LAYER_PIECES):
            settle(side * 4 + zh * 2 + core, piece)
    near_rest(1)
    for side in (x, x_up, x_down, x_far):
        for piece in range(LAYER_PIECES):
            block = side * 4 + zh * 2 + 1 - core
            arrived(block, piece)
            settle(block, piece)
    far_rest(1)
    for side in (x, x_up, x_down, x_far):
        for piece in range(LAYER_PIECES):
            settle(side * 4 + (1 - zh) * 2 + core, piece)
            block = side * 4 + (1 - zh) * 2 + 1 - core
            arrived(block, piece)
            settle(block, piece)

    wsum = wgrad[col]
    for distance in range(1, 16):
        w_copy(distance).wait_recv()
        wsum += w_got[distance - 1]
    wsum_ref[...] = wsum
    for which in (0, 1):
        for place in range(4):
            sib_copy(place, which).wait_send()
            for piece in range(LAYER_PIECES):
                spread_sib(place, which, piece).wait_send()
        for piece in range(LAYER_PIECES):
            far_copy(which, piece).wait_send()
            relay_x(which, piece).wait_send()
            for way in (0, 1):
                near_copy(which, way, piece).wait_send()
                spread_x(which, way, piece).wait_send()
    for piece in range(LAYER_PIECES):
        z_copy(piece).wait_send()
        spread_z(piece).wait_send()
    for distance in range(1, 16):
        w_copy(distance).wait_send()


def dense_layer(count, info, tiles, pairs, weight, bias_vector, out_grad, dst_scale):
    dma = pltpu.SemaphoreType.DMA
    block = block_of(LAYER_PIECES)
    return pl.pallas_call(
        layer_kernel,
        in_specs=[pl.BlockSpec(memory_space=pltpu.SMEM)] * 2 + [VMEM_SPEC] * 6,
        out_specs=[VMEM_SPEC] * 3,
        out_shape=[
            jax.ShapeDtypeStruct((2 * TILE, TILE), F32),
            jax.ShapeDtypeStruct((32, TILE, 2 * TILE), BF16),
            jax.ShapeDtypeStruct(SLICE, F32),
        ],
        scratch_shapes=[
            pltpu.VMEM(tiles.shape, F32),
            pltpu.VMEM((16,) + block, F32),
            pltpu.VMEM((3 * TILE, TILE), BF16),
            pltpu.VMEM((3 * TILE, TILE), BF16),
            pltpu.VMEM((4, 2) + block, F32),
            pltpu.VMEM((2,) + block, F32),
            pltpu.VMEM((2,) + block, F32),
            pltpu.VMEM((2,) + block, F32),
            pltpu.VMEM(block, F32),
            pltpu.VMEM(block, F32),
            pltpu.VMEM((16,) + block, F32),
            pltpu.VMEM((2 * TILE, TILE), F32),
            pltpu.VMEM((2 * TILE, TILE), F32),
            pltpu.VMEM((16,) + SLICE, F32),
            pltpu.VMEM((15,) + SLICE, F32),
            dma((4, 2)), dma((4, 2)), dma((2, LAYER_PIECES)), dma((2, LAYER_PIECES)),
            dma((2, 2, LAYER_PIECES)), dma((2, 2, LAYER_PIECES)), dma((LAYER_PIECES,)), dma((LAYER_PIECES,)),
            dma((16, LAYER_PIECES)), dma((LAYER_PIECES,)), dma((2, 2, LAYER_PIECES)), dma((2, LAYER_PIECES)), dma((4, 2, LAYER_PIECES)),
            dma((15,)), dma((15,)),
        ],
        compiler_params=pltpu.CompilerParams(vmem_limit_bytes=LIMIT, collective_id=1, has_side_effects=True),
        name="dense_layer",
    )(count, info, tiles, pairs, weight, bias_vector.reshape(1, TILE), out_grad, dst_scale)


def scatter_kernel(
    count_ref, info_ref, tiles_ref, source_ref, wsum_ref, scale_ref, grad_ref, wgrad_ref, bgrad_ref,
    sums, part_ref, staged, ring, from_down, from_up, total, line_up, line_down, w_got, w_all,
    far_ssem, far_rsem, near_ssem, near_rsem, line_ssem, line_rsem, w_ssem, w_rsem, all_ssem, all_rsem,
):
    row, col = lax.axis_index("row"), lax.axis_index("col")
    y, z = lax.div(row, 4), lax.rem(row, 4)
    y_up, y_down, y_far = lax.rem(y + 1, 4), lax.rem(y + 3, 4), lax.rem(y + 2, 4)
    wait_for_all = greet(
        [lax.rem(row + d, 16) for d in range(1, 16)], [lax.rem(col + d, 16) for d in range(1, 16)]
    )
    up, down = y_up * 4 + z, y_down * 4 + z

    def far_copy(zb, piece):
        return remote(
            part_ref.at[y_far * 4 + zb, piece], ring.at[zb, piece],
            far_ssem.at[zb, piece], far_rsem.at[zb, piece], row=(up, down)[piece % 2],
        )

    def near_copy(zb, way, piece):
        block = (y_up, y_down)[way] * 4 + zb
        source = staged.at[zb, piece] if piece % 2 == way else part_ref.at[block, piece]
        return remote(
            source, (from_down, from_up)[way].at[zb, piece],
            near_ssem.at[zb, way, piece], near_rsem.at[zb, way, piece], row=(up, down)[way],
        )

    def line_copy(zb, way, piece):
        return remote(
            total.at[zb, piece], (line_up, line_down)[way].at[zb, piece],
            line_ssem.at[zb, piece], line_rsem.at[zb, way, piece],
            row=y * 4 + lax.rem(z + (1 if way == 0 else 3), 4),
        )

    def w_copy(distance):
        return remote(
            wsum_ref, w_got.at[row], w_ssem.at[distance - 1], w_rsem.at[row], row=lax.rem(row + distance, 16)
        )

    def w_arrived(distance):
        sender = lax.rem(row + distance, 16)
        remote(wsum_ref, w_got.at[sender], w_ssem.at[distance - 1], w_rsem.at[sender], row=sender).wait_recv()

    def all_copy(distance):
        return remote(
            w_all.at[col], w_all.at[col], all_ssem.at[distance - 1], all_rsem.at[col], col=lax.rem(col + distance, 16)
        )

    def all_arrived(distance):
        sender = lax.rem(col + distance, 16)
        remote(
            w_all.at[sender], w_all.at[sender], all_ssem.at[distance - 1], all_rsem.at[sender], col=sender
        ).wait_recv()

    def w_total():
        for distance in range(1, 16):
            w_arrived(distance)
        whole = w_got[0]
        for sender in range(1, 16):
            whole += w_got[sender]
        w_all[col] = whole
        for distance in range(1, 16):
            all_copy(distance).start()

    zbs = [in_order(INWARD, place, z) for place in range(4)]

    def far_step(place):
        for piece in range(SCATTER_PIECES):
            far_copy(zbs[place], piece).start()

    def near_step(place, pieces):
        for way in (0, 1):
            for piece in pieces:
                if piece % 2 != way:
                    near_copy(zbs[place], way, piece).start()

    def relay_step(place, pieces):
        zb = zbs[place]
        for piece in pieces:
            way = piece % 2
            far_copy(zb, piece).wait_recv()
            staged[zb, piece] = part_ref[(y_up, y_down)[way] * 4 + zb, piece] + ring[zb, piece]
            near_copy(zb, way, piece).start()

    def line_ways(place):
        zb = zbs[place]
        if place == 3:
            return ((0, z > 0, None), (1, z < 3, None))
        return ((0, (zb > z) & (z > 0), zb > z), (1, (zb < z) & (z < 3), zb < z))

    def close_step(place):
        zb = zbs[place]
        for piece in range(SCATTER_PIECES):
            for way in (0, 1):
                near_copy(zb, way, piece).wait_recv()
            total[zb, piece] = part_ref[y * 4 + zb, piece] + from_down[zb, piece] + from_up[zb, piece]
            for way, comes, goes in line_ways(place):

                @pl.when(comes)
                def _():
                    line_copy(zb, way, piece).wait_recv()
                    total[zb, piece] += (line_up, line_down)[way][zb, piece]

                if goes is not None:
                    pl.when(goes)(lambda: line_copy(zb, way, piece).start())

    def send_step(place):
        zb = zbs[place]
        for piece in range(SCATTER_PIECES):
            far_copy(zb, piece).wait_send()
            for way in (0, 1):
                near_copy(zb, way, piece).wait_send()
        for way, _, goes in line_ways(place):
            for piece in range(SCATTER_PIECES):
                if goes is not None:
                    pl.when(goes)(lambda: line_copy(zb, way, piece).wait_send())

    def product_part(first, last, so_far):
        return block_product(TN, count_ref, info_ref, tiles_ref, source_ref, sums, first, last, so_far)

    groups = tiles_ref.shape[0] // 8
    so_far = product_part(0, groups // 2, jnp.zeros((TILE, TILE), F32))
    wait_for_all()
    for distance in range(1, 16):
        w_copy(distance).start()
    w_got[row] = wsum_ref[...]
    product_part(groups // 2, groups, so_far)
    for place in range(4):
        take_block(info_ref, sums, part_ref, y_far * 4 + zbs[place])
        if place == 0:
            far_step(0)
        for side in (y_up, y_down):
            take_block(info_ref, sums, part_ref, side * 4 + zbs[place])
        if place == 0:
            near_step(0, range(SCATTER_PIECES))
        if place == 1:
            far_step(1)
        take_block(info_ref, sums, part_ref, y * 4 + zbs[place])
    for place in range(4):
        relay_step(place, range(SCATTER_PIECES))
        if place < 3:
            near_step(place + 1, range(SCATTER_PIECES))
        if place < 2:
            far_step(place + 2)
        if place:
            close_step(place - 1)
        if place == 1:
            w_total()
    close_step(3)

    for piece, scale in enumerate(piece_columns(scale_ref, 2 * row, SCATTER_PIECES)):
        grad_ref[pl.ds(piece * scale.shape[0], scale.shape[0]), :] = total[z, piece] * scale
    for distance in range(1, 16):
        all_arrived(distance)
    for part in range(16):
        wgrad_ref[part * 8 : part * 8 + 8, :] = w_all[part, 0:8, :]
    bgrad_ref[...] = w_all[0, 8:9, :]
    for place in range(4):
        send_step(place)
    for distance in range(1, 16):
        w_copy(distance).wait_send()
        all_copy(distance).wait_send()


def scatter_gradients(count, info, tiles, pairs, wsum, src_scale):
    dma = pltpu.SemaphoreType.DMA
    block = block_of(SCATTER_PIECES)
    return pl.pallas_call(
        scatter_kernel,
        in_specs=[pl.BlockSpec(memory_space=pltpu.SMEM)] * 2 + [VMEM_SPEC] * 4,
        out_specs=[VMEM_SPEC] * 3,
        out_shape=[
            jax.ShapeDtypeStruct((2 * TILE, TILE), F32),
            jax.ShapeDtypeStruct((TILE, TILE), F32),
            jax.ShapeDtypeStruct((1, TILE), F32),
        ],
        scratch_shapes=[pltpu.VMEM(tiles.shape, F32), pltpu.VMEM((16,) + block, F32)]
        + [pltpu.VMEM((4,) + block, F32)] * 7
        + [
            pltpu.VMEM((16,) + SLICE, F32),
            pltpu.VMEM((16,) + SLICE, F32),
            dma((4, SCATTER_PIECES)), dma((4, SCATTER_PIECES)), dma((4, 2, SCATTER_PIECES)), dma((4, 2, SCATTER_PIECES)),
            dma((4, SCATTER_PIECES)), dma((4, 2, SCATTER_PIECES)), dma((15,)), dma((16,)), dma((15,)), dma((16,)),
        ],
        compiler_params=pltpu.CompilerParams(vmem_limit_bytes=LIMIT, collective_id=2, has_side_effects=True),
        name="scatter_gradients",
    )(count, info, tiles, pairs, wsum, src_scale)


def put_kernel(*refs):
    count = len(refs) // 2
    ins, outs, sems = refs[:count], refs[count : 2 * count], refs[-1]
    copies = [pltpu.make_async_copy(ins[k], outs[k], sems.at[k]) for k in range(count)]
    for copy in copies:
        copy.start()
    for copy in copies:
        copy.wait()


def put_out(*arrays):
    return pl.pallas_call(
        put_kernel,
        in_specs=[VMEM_SPEC] * len(arrays),
        out_specs=[pl.BlockSpec(memory_space=pltpu.HBM)] * len(arrays),
        out_shape=[jax.ShapeDtypeStruct(array.shape, array.dtype) for array in arrays],
        scratch_shapes=[pltpu.SemaphoreType.DMA((len(arrays),))],
        compiler_params=pltpu.CompilerParams(vmem_limit_bytes=LIMIT),
        name="put_out",
    )(*arrays)


def local(features, weight, bias_vector, out_grad, adj_tiles, tile_slots, tile_counts):
    tiles, pairs, src_scale, dst_scale, forward_info, backward_info = gather_features(
        features, adj_tiles[0, 0], tile_slots[0], tile_counts
    )
    activated, grad_pairs, wsum = dense_layer(
        tile_counts, forward_info, tiles, pairs, weight, bias_vector, out_grad, dst_scale
    )
    feature_grad, weight_grad, bias_grad = scatter_gradients(
        tile_counts, backward_info, tiles, grad_pairs, wsum, src_scale
    )
    activated, feature_grad, weight_grad, bias_grad = put_out(activated, feature_grad, weight_grad, bias_grad)
    return activated, feature_grad, weight_grad, bias_grad.reshape(TILE)


def solution(mesh):
    return jax.shard_map(
        local,
        mesh=mesh,
        in_specs=(
            P(("col", "row"), None),
            P(),
            P(),
            P(("row", "col"), None),
            P("row", "col", None, None, None),
            P("row", "col", None),
            P("row", "col"),
        ),
        out_specs=(P(("row", "col"), None), P(("col", "row"), None), P(), P()),
        check_vma=False,
    )
```

```python
import functools

import jax
import jax.numpy as jnp
from jax import lax
from jax.experimental import pallas as pl
from jax.experimental.pallas import tpu as pltpu
from jax.sharding import PartitionSpec as P

TILE = 128
MESH = pl.DeviceIdType.MESH
F32 = jnp.float32
BF16 = jnp.bfloat16
HIGHEST = lax.Precision.HIGHEST
VMEM_SPEC = pl.BlockSpec(memory_space=pltpu.VMEM)
CHUNK = 8
LIMIT = 24 << 20
GATHER_PIECES = 2
LAYER_PIECES = 2
SCATTER_PIECES = 2


def block_of(pieces):
    return (pieces, 2 * TILE // pieces, TILE)


def by_way(pieces):
    return [(piece % 2, piece) for piece in range(pieces)] + [(piece % 2, piece + 1 - 2 * (piece % 2)) for piece in range(pieces)]


def piece_columns(scale_ref, first, pieces):
    columns = [to_column(scale_ref[pl.ds(first + half, 1), :]) for half in (0, 1)]
    each = pieces // 2
    rows = TILE // each
    return [columns[k // each][k % each * rows : (k % each + 1) * rows] for k in range(pieces)]
NT = (((1,), (1,)), ((), ()))
NN = (((1,), (0,)), ((), ()))
TN = (((0,), (0,)), ((), ()))


def remote(src, dst, send_sem, recv_sem, **where):
    return pltpu.make_async_remote_copy(
        src_ref=src,
        dst_ref=dst,
        send_sem=send_sem,
        recv_sem=recv_sem,
        device_id=where,
        device_id_type=MESH,
    )


def xor_peer(index, bit):
    return index + bit - 2 * bit * lax.rem(lax.div(index, bit), 2)


def greet(rows, cols):
    barrier = pltpu.get_barrier_semaphore()
    for peer in rows:
        pl.semaphore_signal(barrier, inc=1, device_id={"row": peer}, device_id_type=MESH)
    for peer in cols:
        pl.semaphore_signal(barrier, inc=1, device_id={"col": peer}, device_id_type=MESH)
    return lambda: pl.semaphore_wait(barrier, len(rows) + len(cols))


def to_column(row_vector):
    spread = jnp.broadcast_to(row_vector, (TILE, TILE))
    diagonal = lax.broadcasted_iota(jnp.int32, (TILE, TILE), 0) == lax.broadcasted_iota(
        jnp.int32, (TILE, TILE), 1
    )
    return jnp.sum(jnp.where(diagonal, spread, 0.0), axis=1, keepdims=True)


def split_pair(value):
    high = value.astype(BF16)
    low = (value - high.astype(F32)).astype(BF16)
    return jnp.concatenate([high, low], axis=1)


def put_pair(pair_ref, block, piece, pieces, value):
    each = pieces // 2
    rows = TILE // each
    here = slice(piece % each * rows, (piece % each + 1) * rows)
    pair_ref[2 * block + piece // each, here, :] = split_pair(value)


def sort_table(slots, live, by_row):
    tile_row = jnp.floor(slots * (1.0 / 32.0))
    tile_col = slots - 32.0 * tile_row
    lane = lax.broadcasted_iota(jnp.int32, (1, TILE), 1).astype(F32)
    key = jnp.where(live, tile_row * 32.0 + tile_col if by_row else tile_col * 32.0 + tile_row, 2048.0 + lane)
    key_column = to_column(key)
    rank = jnp.sum(jnp.where(key < key_column, 1.0, 0.0), axis=1, keepdims=True)
    place = rank == lax.broadcasted_iota(jnp.int32, (TILE, TILE), 1).astype(F32)
    number = lax.broadcasted_iota(jnp.int32, (TILE, 1), 0).astype(F32)

    def moved(column):
        return jnp.sum(jnp.where(place, column, 0.0), axis=0, keepdims=True).astype(jnp.int32)

    ends = (to_column(tile_row), to_column(tile_col))
    if not by_row:
        ends = ends[::-1]
    live_column = to_column(jnp.where(live, 1.0, 0.0))
    target = lax.broadcasted_iota(jnp.int32, (TILE, TILE), 1).astype(F32)

    def counted(which):
        return jnp.sum(jnp.where(which, live_column, 0.0), axis=0, keepdims=True).astype(jnp.int32)

    return moved(number), moved(ends[0]), moved(ends[1]), counted(ends[0] < target), counted(ends[0] <= target)


def block_product(dims, count_ref, info_ref, tiles_ref, pair_ref, sums_ref, first, last, total):
    unroll = 8
    count = count_ref[0, 0]

    def body(step, total):
        for u in range(unroll):
            k = step * unroll + u
            at = jnp.clip(count - 1, 0, k)
            number = jnp.clip(info_ref[0, at], 0, tiles_ref.shape[0] - 1)
            source = jnp.clip(info_ref[2, at], 0, pair_ref.shape[0] - 1)
            both = lax.dot_general(tiles_ref[number], pair_ref[source], dims, preferred_element_type=F32)
            goes_on = (k > 0) & (info_ref[1, jnp.maximum(at - 1, 0)] == info_ref[1, at])
            total = both[:, :TILE] + both[:, TILE:] + jnp.where(goes_on, total, 0.0)
            sums_ref[k] = total
        return total

    return lax.fori_loop(first, last, body, total)


def take_block(info_ref, sums_ref, part_ref, block):
    rows = part_ref.shape[2]
    each = TILE // rows
    for half in (0, 1):
        first, end = info_ref[3, 2 * block + half], info_ref[4, 2 * block + half]
        tile = jnp.where(end > first, sums_ref[jnp.clip(end - 1, 0, sums_ref.shape[0] - 1)], 0.0)
        for k in range(each):
            part_ref[block, half * each + k] = tile[k * rows : (k + 1) * rows]


def split_rows(value, order):
    high = value.astype(BF16)
    low = (value - high.astype(F32)).astype(BF16)
    return jnp.concatenate([(high, low)[k] for k in order], axis=0)


def split_columns(value):
    high = value.astype(BF16)
    low = (value - high.astype(F32)).astype(BF16)
    return jnp.concatenate([high, low, high], axis=1)


OUTWARD = ((0, 1, 2, 3), (1, 0, 2, 3), (2, 1, 3, 0), (3, 2, 1, 0))
INWARD = tuple(order[::-1] for order in OUTWARD)


def in_order(orders, place, z):
    low, high = lax.rem(z, 2), lax.div(z, 2)
    v = [orders[k][place] for k in range(4)]
    return v[0] + (v[1] - v[0]) * low + (v[2] - v[0]) * high + (v[3] - v[2] - v[1] + v[0]) * low * high


def gather_kernel(
    count_ref, slots_ref, feat_ref, adj_ref,
    tiles_ref, pair_ref, src_scale_ref, dst_scale_ref, forward_info_ref, backward_info_ref,
    adj_got, row_sums, col_sums, parts, held, slots_got, deg_sent, deg_got,
    feat_sem, adj_sem, recv_sem, z_sem, y_sem, relay_sem, deg_send_sem, deg_recv_sem,
):
    chunks = adj_ref.shape[0] // CHUNK
    row, col = lax.axis_index("row"), lax.axis_index("col")
    y, z = lax.div(row, 4), lax.rem(row, 4)
    y_up, y_down, y_far = lax.rem(y + 1, 4), lax.rem(y + 3, 4), lax.rem(y + 2, 4)
    wait_for_all = greet(
        [lax.rem(y + d, 4) * 4 + z for d in (1, 2, 3)] + [y * 4 + lax.rem(z + d, 4) for d in (1, 2, 3)],
        [xor_peer(col, bit) for bit in (1, 2, 4, 8)],
    )

    def adj_copy(chunk):
        here = pl.ds(pl.multiple_of(chunk * CHUNK, CHUNK), CHUNK)
        return pltpu.make_async_copy(adj_ref.at[here], adj_got.at[here], adj_sem.at[chunk])

    feat_copy = pltpu.make_async_copy(feat_ref, held.at[row], feat_sem.at[0])
    feat_copy.start()
    slots_copy = pltpu.make_async_copy(slots_ref, slots_got, feat_sem.at[1])
    slots_copy.start()
    for chunk in range(chunks):
        adj_copy(chunk).start()

    ones = jnp.ones((TILE, TILE), F32).astype(BF16)
    diagonal = lax.broadcasted_iota(jnp.int32, (TILE, TILE), 0) == lax.broadcasted_iota(
        jnp.int32, (TILE, TILE), 1
    )

    def degree_chunks(first, last):
        def body(chunk, carry):
            adj_copy(chunk).wait()
            for k in range(CHUNK):
                slot = chunk * CHUNK + k
                tile = adj_got[slot].astype(F32)
                narrow = tile.astype(BF16)
                tiles_ref[slot] = narrow
                col_sums[pl.ds(slot, 1), :] = jnp.sum(tile, axis=0, keepdims=True)
                sums = jnp.dot(narrow, ones, preferred_element_type=F32)
                row_sums[pl.ds(slot, 1), :] = jnp.sum(jnp.where(diagonal, sums, 0.0), axis=0, keepdims=True)
            return carry

        lax.fori_loop(first, last, body, 0)

    slots_copy.wait()
    slots = slots_got[...].astype(F32)
    live = lax.broadcasted_iota(jnp.int32, (1, TILE), 1) < count_ref[0, 0]

    def degree_parts():
        tile_row = jnp.floor(slots * (1.0 / 32.0))
        tile_col = slots - 32.0 * tile_row
        tile_number = lax.broadcasted_iota(jnp.int32, (32, TILE), 0).astype(F32)
        row_select = jnp.where(live & (tile_row == tile_number), 1.0, 0.0).astype(BF16)
        col_select = jnp.where(live & (tile_col == tile_number), 1.0, 0.0).astype(BF16)
        parts[0] = jnp.dot(col_select, col_sums[...].astype(BF16), preferred_element_type=F32)
        parts[1] = jnp.dot(row_select, row_sums[...].astype(BF16), preferred_element_type=F32)

    def z_copy(z_from, way, piece):
        block = y * 4 + z_from
        return remote(
            held.at[block, piece], held.at[block, piece],
            z_sem.at[z_from, way, piece], recv_sem.at[block, piece],
            row=y * 4 + lax.rem(z + (1 if way == 0 else 3), 4),
        )

    def y_copy(z_from, way, piece):
        block = y * 4 + z_from
        return remote(
            held.at[block, piece], held.at[block, piece],
            y_sem.at[z_from, way, piece], recv_sem.at[block, piece],
            row=(y_up, y_down)[way] * 4 + z,
        )

    def relay_copy(z_from, piece):
        way = piece % 2
        block = (y_down, y_up)[way] * 4 + z_from
        return remote(
            held.at[block, piece], held.at[block, piece],
            relay_sem.at[z_from, piece], recv_sem.at[block, piece],
            row=(y_up, y_down)[way] * 4 + z,
        )

    def arrived(block, piece):
        remote(
            held.at[block, piece], held.at[block, piece], relay_sem.at[0, piece], recv_sem.at[block, piece],
            row=y_up * 4 + z,
        ).wait_recv()

    def on_line(place, pieces, action):
        z_from = in_order(OUTWARD, place, z)
        for way in (0, 1):
            goes = z < 3 if way == 0 else z > 0
            if place:
                goes = goes & (z_from < z if way == 0 else z_from > z)

            @pl.when(goes)
            def _():
                for piece in pieces:
                    action(z_copy(z_from, way, piece))

    def column_step(place):
        z_from = in_order(OUTWARD, place, z)
        if place:
            for piece in range(GATHER_PIECES):
                arrived(y * 4 + z_from, piece)
        on_line(place, range(GATHER_PIECES), lambda copy: copy.start())
        for way, piece in by_way(GATHER_PIECES):
            y_copy(z_from, way, piece).start()

    def relay_step(place):
        z_from = in_order(OUTWARD, place, z)
        for piece in range(GATHER_PIECES):
            arrived((y_down, y_up)[piece % 2] * 4 + z_from, piece)
            relay_copy(z_from, piece).start()

    def degree_source(which, step):
        return parts.at[which] if step == 0 else deg_sent.at[which, step - 1]

    def degree_copy(which, step):
        where = {("row", "col")[which]: xor_peer((row, col)[which], 1 << step)}
        return remote(
            degree_source(which, step), deg_got.at[which, step],
            deg_send_sem.at[which, step], deg_recv_sem.at[which, step], **where
        )

    def degree_step(step):
        for which in (0, 1):
            degree_copy(which, step).wait_recv()
            deg_sent[which, step] = degree_source(which, step)[...] + deg_got[which, step]
            if step < 3:
                degree_copy(which, step + 1).start()

    feat_copy.wait()
    wait_for_all()
    column_step(0)
    degree_chunks(0, chunks // 2)
    relay_step(0)
    column_step(1)
    degree_chunks(chunks // 2, chunks)
    degree_parts()
    for which in (0, 1):
        degree_copy(which, 0).start()
    relay_step(1)
    column_step(2)
    degree_step(0)
    relay_step(2)
    degree_step(1)
    column_step(3)
    degree_step(2)
    for info_ref, by_row in ((forward_info_ref, True), (backward_info_ref, False)):
        for place, line in enumerate(sort_table(slots, live, by_row)):
            info_ref[place : place + 1, :] = line
    relay_step(3)
    degree_step(3)

    src_scale_ref[...] = lax.rsqrt(1.0 + deg_sent[0, 3])
    dst_scale_ref[...] = lax.rsqrt(1.0 + deg_sent[1, 3])

    def settle(block):
        for piece, scale in enumerate(piece_columns(src_scale_ref, 2 * block, GATHER_PIECES)):
            put_pair(pair_ref, block, piece, GATHER_PIECES, held[block, piece] * scale)

    for place in range(4):
        settle(y * 4 + in_order(OUTWARD, place, z))
    for place in range(4):
        z_from = in_order(OUTWARD, place, z)
        for way in (0, 1):
            block = (y_down, y_up)[way] * 4 + z_from
            for piece in range(1 - way, GATHER_PIECES, 2):
                arrived(block, piece)
            settle(block)
    for place in range(4):
        z_from = in_order(OUTWARD, place, z)
        for piece in range(GATHER_PIECES):
            arrived(y_far * 4 + z_from, piece)
        settle(y_far * 4 + z_from)
    for place in range(4):
        z_from = in_order(OUTWARD, place, z)
        for piece in range(GATHER_PIECES):
            for way in (0, 1):
                y_copy(z_from, way, piece).wait_send()
            relay_copy(z_from, piece).wait_send()
        on_line(place, range(GATHER_PIECES), lambda copy: copy.wait_send())
    for which in (0, 1):
        for step in range(4):
            degree_copy(which, step).wait_send()


def gather_features(features, adj_tiles, slots, count):
    dma = pltpu.SemaphoreType.DMA
    slot_total = adj_tiles.shape[0]
    return pl.pallas_call(
        gather_kernel,
        in_specs=[
            pl.BlockSpec(memory_space=pltpu.SMEM),
            pl.BlockSpec(memory_space=pltpu.HBM),
            pl.BlockSpec(memory_space=pltpu.HBM),
            pl.BlockSpec(memory_space=pltpu.HBM),
        ],
        out_specs=[VMEM_SPEC] * 6,
        out_shape=[
            jax.ShapeDtypeStruct((slot_total, TILE, TILE), BF16),
            jax.ShapeDtypeStruct((32, TILE, 2 * TILE), BF16),
            jax.ShapeDtypeStruct((32, TILE), F32),
            jax.ShapeDtypeStruct((32, TILE), F32),
            jax.ShapeDtypeStruct((5, TILE), jnp.int32),
            jax.ShapeDtypeStruct((5, TILE), jnp.int32),
        ],
        scratch_shapes=[
            pltpu.VMEM((slot_total, TILE, TILE), jnp.int32),
            pltpu.VMEM((slot_total, TILE), F32),
            pltpu.VMEM((slot_total, TILE), F32),
            pltpu.VMEM((2, 32, TILE), F32),
            pltpu.VMEM((16,) + block_of(GATHER_PIECES), F32),
            pltpu.VMEM((1, TILE), jnp.int32),
            pltpu.VMEM((2, 4, 32, TILE), F32),
            pltpu.VMEM((2, 4, 32, TILE), F32),
            dma((2,)),
            dma((slot_total // CHUNK,)),
            dma((16, GATHER_PIECES)),
            dma((4, 2, GATHER_PIECES)),
            dma((4, 2, GATHER_PIECES)),
            dma((4, GATHER_PIECES)),
            dma((2, 4)),
            dma((2, 4)),
        ],
        compiler_params=pltpu.CompilerParams(vmem_limit_bytes=LIMIT, collective_id=0, has_side_effects=True),
        name="gather_features",
    )(
        count,
        pltpu.with_memory_space_constraint(slots, pltpu.HBM),
        pltpu.with_memory_space_constraint(features.reshape(block_of(GATHER_PIECES)), pltpu.HBM),
        pltpu.with_memory_space_constraint(adj_tiles, pltpu.HBM),
    )


SLICE = (16, TILE)


def layer_kernel(
    count_ref, info_ref, tiles_ref, source_ref, w_ref, b_ref, grad_ref, scale_ref, act_ref, pair_ref, wsum_ref,
    sums, part_ref, w_fore, w_back, sib_got, ring, from_left, from_right, z_sent, z_got, held, aggs, grads, wgrad, w_got,
    sib_ssem, sib_rsem, far_ssem, far_rsem, near_ssem, near_rsem, z_ssem, z_rsem,
    recv_sem, zg_sem, xg_sem, relay_sem, sg_sem, w_ssem, w_rsem,
):
    col = lax.axis_index("col")
    x, zh, core = lax.div(col, 4), lax.rem(lax.div(col, 2), 2), lax.rem(col, 2)
    x_up, x_down, x_far = lax.rem(x + 1, 4), lax.rem(x + 3, 4), lax.rem(x + 2, 4)
    sibling = col + 1 - 2 * core
    z_peer = col + 2 - 4 * zh
    up, down = x_up * 4 + zh * 2 + core, x_down * 4 + zh * 2 + core
    wait_for_all = greet([], [lax.rem(col + d, 16) for d in range(1, 16)])
    block_product(
        NN, count_ref, info_ref, tiles_ref, source_ref, sums, 0, tiles_ref.shape[0] // 8, jnp.zeros((TILE, TILE), F32)
    )
    w_fore[...] = split_rows(w_ref[...], (0, 0, 1))
    w_back[...] = split_rows(jnp.transpose(w_ref[...]), (0, 0, 1))
    first, rest = (0, 1), range(2, LAYER_PIECES)
    after = [(piece % 2, piece + 1 - 2 * (piece % 2)) for piece in rest]

    def sib_copy(place, which):
        target = (x_far, x_up, x_down, x)[place]
        half_z = 1 - zh if which == 0 else zh
        return remote(
            part_ref.at[target * 4 + half_z * 2 + 1 - core], sib_got.at[place, which],
            sib_ssem.at[place, which], sib_rsem.at[place, which], col=sibling,
        )

    def far_copy(which, piece):
        return remote(
            sib_got.at[0, which, piece], ring.at[which, piece],
            far_ssem.at[which, piece], far_rsem.at[which, piece], col=(up, down)[piece % 2],
        )

    def near_copy(which, way, piece):
        return remote(
            sib_got.at[1 + way, which, piece], (from_left, from_right)[way].at[which, piece],
            near_ssem.at[which, way, piece], near_rsem.at[which, way, piece], col=(up, down)[way],
        )

    def z_copy(piece):
        return remote(z_sent.at[piece], z_got.at[piece], z_ssem.at[piece], z_rsem.at[piece], col=z_peer)

    def join(place, which):
        target = (x_far, x_up, x_down, x)[place]
        half_z = 1 - zh if which == 0 else zh
        sib_copy(place, which).wait_recv()
        sib_got[place, which] += part_ref[target * 4 + half_z * 2 + core]

    def open_ring(which):
        join(0, which)
        for piece in range(LAYER_PIECES):
            far_copy(which, piece).start()
        for way in (0, 1):
            join(1 + way, which)
            near_copy(which, way, 1 - way).start()
        join(3, which)

    def relay_ring(which, pieces):
        for piece in pieces:
            way = piece % 2
            far_copy(which, piece).wait_recv()
            sib_got[1 + way, which, piece] += ring[which, piece]
            near_copy(which, way, piece).start()

    def rest_ring(which):
        for way, piece in after:
            near_copy(which, way, piece).start()

    def ring_total(which, piece):
        for way in (0, 1):
            near_copy(which, way, piece).wait_recv()
        return sib_got[3, which, piece] + from_left[which, piece] + from_right[which, piece]

    def send_over(pieces):
        for piece in pieces:
            z_sent[piece] = ring_total(0, piece)
            z_copy(piece).start()

    wait_for_all()
    for which in (0, 1):
        for place in range(4):
            target = (x_far, x_up, x_down, x)[place] * 4 + (1 - zh if which == 0 else zh) * 2
            take_block(info_ref, sums, part_ref, target + 1 - core)
            sib_copy(place, which).start()
            take_block(info_ref, sums, part_ref, target + core)
    open_ring(0)
    relay_ring(0, first)
    rest_ring(0)
    relay_ring(0, rest)
    open_ring(1)
    send_over(first)
    relay_ring(1, first)
    rest_ring(1)
    send_over(rest)
    relay_ring(1, rest)

    def spread_z(piece):
        return remote(
            held.at[col, piece], held.at[col, piece], zg_sem.at[piece], recv_sem.at[col, piece], col=z_peer
        )

    def spread_x(which, way, piece):
        half_z = zh if which == 0 else 1 - zh
        block = x * 4 + half_z * 2 + core
        return remote(
            held.at[block, piece], held.at[block, piece], xg_sem.at[which, way, piece], recv_sem.at[block, piece],
            col=(up, down)[way],
        )

    def relay_x(which, piece):
        half_z = zh if which == 0 else 1 - zh
        way = piece % 2
        block = (x_down, x_up)[way] * 4 + half_z * 2 + core
        return remote(
            held.at[block, piece], held.at[block, piece], relay_sem.at[which, piece], recv_sem.at[block, piece],
            col=(up, down)[way],
        )

    def spread_sib(place, which, piece):
        target = (x, x_up, x_down, x_far)[place]
        half_z = zh if which == 0 else 1 - zh
        block = target * 4 + half_z * 2 + core
        return remote(
            held.at[block, piece], held.at[block, piece], sg_sem.at[place, which, piece], recv_sem.at[block, piece],
            col=sibling,
        )

    def arrived(block, piece):
        remote(
            held.at[block, piece], held.at[block, piece], zg_sem.at[piece], recv_sem.at[block, piece], col=sibling
        ).wait_recv()

    def spread(which, piece):
        way = piece % 2
        spread_x(which, way, piece).start()
        spread_x(which, 1 - way, piece).start()
        spread_sib(0, which, piece).start()

    def settle(block, piece):
        put_pair(pair_ref, block, piece, LAYER_PIECES, held[block, piece])

    for piece, scale in enumerate(piece_columns(scale_ref, 2 * col, LAYER_PIECES)):
        here = slice(piece * part_ref.shape[2], (piece + 1) * part_ref.shape[2])
        own = ring_total(1, piece)
        z_copy(piece).wait_recv()
        aggregated = (own + z_got[piece]) * scale
        preact = jnp.dot(split_columns(aggregated), w_fore[...], preferred_element_type=F32) + b_ref[...]
        logistic = 1.0 / (1.0 + jnp.exp(-preact))
        pre_grad = grad_ref[here, :] * logistic * (1.0 + preact * (1.0 - logistic))
        held[col, piece] = scale * jnp.dot(split_columns(pre_grad), w_back[...], preferred_element_type=F32)
        spread_z(piece).start()
        spread(0, piece)
        act_ref[here, :] = preact * logistic
        aggs[here, :] = aggregated
        grads[here, :] = pre_grad

    weight_part = lax.dot_general(
        split_rows(aggs[...], (0, 1, 0)), split_rows(grads[...], (0, 0, 1)), TN, preferred_element_type=F32
    )
    bias_part = jnp.broadcast_to(jnp.sum(grads[...], axis=0, keepdims=True), (8, TILE))
    for part in range(16):
        wgrad[part, 0:8, :] = weight_part[part * 8 : part * 8 + 8]
        wgrad[part, 8:16, :] = bias_part

    def w_copy(distance):
        peer = lax.rem(col + distance, 16)
        return remote(
            wgrad.at[peer], w_got.at[distance - 1], w_ssem.at[distance - 1], w_rsem.at[distance - 1], col=peer
        )

    for distance in range(1, 16):
        w_copy(distance).start()

    def relay(which, pieces):
        half_z = zh if which == 0 else 1 - zh
        for piece in pieces:
            way = piece % 2
            arrived((x_down, x_up)[way] * 4 + half_z * 2 + core, piece)
            relay_x(which, piece).start()
            spread_sib((2, 1)[way], which, piece).start()

    def near_rest(which):
        half_z = zh if which == 0 else 1 - zh
        for piece in range(LAYER_PIECES):
            way = piece % 2
            arrived((x_up, x_down)[way] * 4 + half_z * 2 + core, piece)
            spread_sib((1, 2)[way], which, piece).start()

    def far_rest(which):
        half_z = zh if which == 0 else 1 - zh
        for piece in range(LAYER_PIECES):
            arrived(x_far * 4 + half_z * 2 + core, piece)
            spread_sib(3, which, piece).start()

    other = x * 4 + (1 - zh) * 2 + core

    def take_over(piece):
        arrived(other, piece)
        spread(1, piece)

    relay(0, range(LAYER_PIECES))
    near_rest(0)
    for piece in range(LAYER_PIECES):
        take_over(piece)
        if piece == 1:
            far_rest(0)
        if piece >= 2:
            relay(1, (piece - 2,))
    for piece in range(max(LAYER_PIECES - 2, 0), LAYER_PIECES - 1):
        relay(1, (piece,))
    for side in (x, x_up):
        for piece in range(LAYER_PIECES):
            settle(side * 4 + zh * 2 + core, piece)
    relay(1, (LAYER_PIECES - 1,))
    for side in (x_down, x_far):
        for piece in range(LAYER_PIECES):
            settle(side * 4 + zh * 2 + core, piece)
    near_rest(1)
    for side in (x, x_up, x_down, x_far):
        for piece in range(LAYER_PIECES):
            block = side * 4 + zh * 2 + 1 - core
            arrived(block, piece)
            settle(block, piece)
    far_rest(1)
    for side in (x, x_up, x_down, x_far):
        for piece in range(LAYER_PIECES):
            settle(side * 4 + (1 - zh) * 2 + core, piece)
            block = side * 4 + (1 - zh) * 2 + 1 - core
            arrived(block, piece)
            settle(block, piece)

    wsum = wgrad[col]
    for distance in range(1, 16):
        w_copy(distance).wait_recv()
        wsum += w_got[distance - 1]
    wsum_ref[...] = wsum
    for which in (0, 1):
        for place in range(4):
            sib_copy(place, which).wait_send()
            for piece in range(LAYER_PIECES):
                spread_sib(place, which, piece).wait_send()
        for piece in range(LAYER_PIECES):
            far_copy(which, piece).wait_send()
            relay_x(which, piece).wait_send()
            for way in (0, 1):
                near_copy(which, way, piece).wait_send()
                spread_x(which, way, piece).wait_send()
    for piece in range(LAYER_PIECES):
        z_copy(piece).wait_send()
        spread_z(piece).wait_send()
    for distance in range(1, 16):
        w_copy(distance).wait_send()


def dense_layer(count, info, tiles, pairs, weight, bias_vector, out_grad, dst_scale):
    dma = pltpu.SemaphoreType.DMA
    block = block_of(LAYER_PIECES)
    return pl.pallas_call(
        layer_kernel,
        in_specs=[pl.BlockSpec(memory_space=pltpu.SMEM)] * 2 + [VMEM_SPEC] * 6,
        out_specs=[VMEM_SPEC] * 3,
        out_shape=[
            jax.ShapeDtypeStruct((2 * TILE, TILE), F32),
            jax.ShapeDtypeStruct((32, TILE, 2 * TILE), BF16),
            jax.ShapeDtypeStruct(SLICE, F32),
        ],
        scratch_shapes=[
            pltpu.VMEM(tiles.shape, F32),
            pltpu.VMEM((16,) + block, F32),
            pltpu.VMEM((3 * TILE, TILE), BF16),
            pltpu.VMEM((3 * TILE, TILE), BF16),
            pltpu.VMEM((4, 2) + block, F32),
            pltpu.VMEM((2,) + block, F32),
            pltpu.VMEM((2,) + block, F32),
            pltpu.VMEM((2,) + block, F32),
            pltpu.VMEM(block, F32),
            pltpu.VMEM(block, F32),
            pltpu.VMEM((16,) + block, F32),
            pltpu.VMEM((2 * TILE, TILE), F32),
            pltpu.VMEM((2 * TILE, TILE), F32),
            pltpu.VMEM((16,) + SLICE, F32),
            pltpu.VMEM((15,) + SLICE, F32),
            dma((4, 2)), dma((4, 2)), dma((2, LAYER_PIECES)), dma((2, LAYER_PIECES)),
            dma((2, 2, LAYER_PIECES)), dma((2, 2, LAYER_PIECES)), dma((LAYER_PIECES,)), dma((LAYER_PIECES,)),
            dma((16, LAYER_PIECES)), dma((LAYER_PIECES,)), dma((2, 2, LAYER_PIECES)), dma((2, LAYER_PIECES)), dma((4, 2, LAYER_PIECES)),
            dma((15,)), dma((15,)),
        ],
        compiler_params=pltpu.CompilerParams(vmem_limit_bytes=LIMIT, collective_id=1, has_side_effects=True),
        name="dense_layer",
    )(count, info, tiles, pairs, weight, bias_vector.reshape(1, TILE), out_grad, dst_scale)


def scatter_kernel(
    count_ref, info_ref, tiles_ref, source_ref, wsum_ref, scale_ref, grad_ref, wgrad_ref, bgrad_ref,
    sums, part_ref, staged, ring, from_down, from_up, total, line_up, line_down, w_got, w_all,
    far_ssem, far_rsem, near_ssem, near_rsem, line_ssem, line_rsem, w_ssem, w_rsem, all_ssem, all_rsem,
):
    row, col = lax.axis_index("row"), lax.axis_index("col")
    y, z = lax.div(row, 4), lax.rem(row, 4)
    y_up, y_down, y_far = lax.rem(y + 1, 4), lax.rem(y + 3, 4), lax.rem(y + 2, 4)
    wait_for_all = greet(
        [lax.rem(row + d, 16) for d in range(1, 16)], [lax.rem(col + d, 16) for d in range(1, 16)]
    )
    up, down = y_up * 4 + z, y_down * 4 + z

    def far_copy(zb, piece):
        return remote(
            part_ref.at[y_far * 4 + zb, piece], ring.at[zb, piece],
            far_ssem.at[zb, piece], far_rsem.at[zb, piece], row=(up, down)[piece % 2],
        )

    def near_copy(zb, way, piece):
        block = (y_up, y_down)[way] * 4 + zb
        source = staged.at[zb, piece] if piece % 2 == way else part_ref.at[block, piece]
        return remote(
            source, (from_down, from_up)[way].at[zb, piece],
            near_ssem.at[zb, way, piece], near_rsem.at[zb, way, piece], row=(up, down)[way],
        )

    def line_copy(zb, way, piece):
        return remote(
            total.at[zb, piece], (line_up, line_down)[way].at[zb, piece],
            line_ssem.at[zb, piece], line_rsem.at[zb, way, piece],
            row=y * 4 + lax.rem(z + (1 if way == 0 else 3), 4),
        )

    def w_copy(distance):
        return remote(
            wsum_ref, w_got.at[row], w_ssem.at[distance - 1], w_rsem.at[row], row=lax.rem(row + distance, 16)
        )

    def w_arrived(distance):
        sender = lax.rem(row + distance, 16)
        remote(wsum_ref, w_got.at[sender], w_ssem.at[distance - 1], w_rsem.at[sender], row=sender).wait_recv()

    def all_copy(distance):
        return remote(
            w_all.at[col], w_all.at[col], all_ssem.at[distance - 1], all_rsem.at[col], col=lax.rem(col + distance, 16)
        )

    def all_arrived(distance):
        sender = lax.rem(col + distance, 16)
        remote(
            w_all.at[sender], w_all.at[sender], all_ssem.at[distance - 1], all_rsem.at[sender], col=sender
        ).wait_recv()

    def w_total():
        for distance in range(1, 16):
            w_arrived(distance)
        whole = w_got[0]
        for sender in range(1, 16):
            whole += w_got[sender]
        w_all[col] = whole
        for distance in range(1, 16):
            all_copy(distance).start()

    zbs = [in_order(INWARD, place, z) for place in range(4)]

    def far_step(place):
        for piece in range(SCATTER_PIECES):
            far_copy(zbs[place], piece).start()

    def near_step(place, pieces):
        for way in (0, 1):
            for piece in pieces:
                if piece % 2 != way:
                    near_copy(zbs[place], way, piece).start()

    def relay_step(place, pieces):
        zb = zbs[place]
        for piece in pieces:
            way = piece % 2
            far_copy(zb, piece).wait_recv()
            staged[zb, piece] = part_ref[(y_up, y_down)[way] * 4 + zb, piece] + ring[zb, piece]
            near_copy(zb, way, piece).start()

    def line_ways(place):
        zb = zbs[place]
        if place == 3:
            return ((0, z > 0, None), (1, z < 3, None))
        return ((0, (zb > z) & (z > 0), zb > z), (1, (zb < z) & (z < 3), zb < z))

    def close_step(place):
        zb = zbs[place]
        for piece in range(SCATTER_PIECES):
            for way in (0, 1):
                near_copy(zb, way, piece).wait_recv()
            total[zb, piece] = part_ref[y * 4 + zb, piece] + from_down[zb, piece] + from_up[zb, piece]
            for way, comes, goes in line_ways(place):

                @pl.when(comes)
                def _():
                    line_copy(zb, way, piece).wait_recv()
                    total[zb, piece] += (line_up, line_down)[way][zb, piece]

                if goes is not None:
                    pl.when(goes)(lambda: line_copy(zb, way, piece).start())

    def send_step(place):
        zb = zbs[place]
        for piece in range(SCATTER_PIECES):
            far_copy(zb, piece).wait_send()
            for way in (0, 1):
                near_copy(zb, way, piece).wait_send()
        for way, _, goes in line_ways(place):
            for piece in range(SCATTER_PIECES):
                if goes is not None:
                    pl.when(goes)(lambda: line_copy(zb, way, piece).wait_send())

    def product_part(first, last, so_far):
        return block_product(TN, count_ref, info_ref, tiles_ref, source_ref, sums, first, last, so_far)

    groups = tiles_ref.shape[0] // 8
    so_far = product_part(0, groups // 2, jnp.zeros((TILE, TILE), F32))
    wait_for_all()
    for distance in range(1, 16):
        w_copy(distance).start()
    w_got[row] = wsum_ref[...]
    product_part(groups // 2, groups, so_far)
    for place in range(4):
        take_block(info_ref, sums, part_ref, y_far * 4 + zbs[place])
        if place == 0:
            far_step(0)
        for side in (y_up, y_down):
            take_block(info_ref, sums, part_ref, side * 4 + zbs[place])
        if place == 0:
            near_step(0, range(SCATTER_PIECES))
        if place == 1:
            far_step(1)
        take_block(info_ref, sums, part_ref, y * 4 + zbs[place])
    for place in range(4):
        relay_step(place, range(SCATTER_PIECES))
        if place < 3:
            near_step(place + 1, range(SCATTER_PIECES))
        if place < 2:
            far_step(place + 2)
        if place:
            close_step(place - 1)
        if place == 2:
            w_total()
    close_step(3)

    for piece, scale in enumerate(piece_columns(scale_ref, 2 * row, SCATTER_PIECES)):
        grad_ref[pl.ds(piece * scale.shape[0], scale.shape[0]), :] = total[z, piece] * scale
    for distance in range(1, 16):
        all_arrived(distance)
    for part in range(16):
        wgrad_ref[part * 8 : part * 8 + 8, :] = w_all[part, 0:8, :]
    bgrad_ref[...] = w_all[0, 8:9, :]
    for place in range(4):
        send_step(place)
    for distance in range(1, 16):
        w_copy(distance).wait_send()
        all_copy(distance).wait_send()


def scatter_gradients(count, info, tiles, pairs, wsum, src_scale):
    dma = pltpu.SemaphoreType.DMA
    block = block_of(SCATTER_PIECES)
    return pl.pallas_call(
        scatter_kernel,
        in_specs=[pl.BlockSpec(memory_space=pltpu.SMEM)] * 2 + [VMEM_SPEC] * 4,
        out_specs=[VMEM_SPEC] * 3,
        out_shape=[
            jax.ShapeDtypeStruct((2 * TILE, TILE), F32),
            jax.ShapeDtypeStruct((TILE, TILE), F32),
            jax.ShapeDtypeStruct((1, TILE), F32),
        ],
        scratch_shapes=[pltpu.VMEM(tiles.shape, F32), pltpu.VMEM((16,) + block, F32)]
        + [pltpu.VMEM((4,) + block, F32)] * 7
        + [
            pltpu.VMEM((16,) + SLICE, F32),
            pltpu.VMEM((16,) + SLICE, F32),
            dma((4, SCATTER_PIECES)), dma((4, SCATTER_PIECES)), dma((4, 2, SCATTER_PIECES)), dma((4, 2, SCATTER_PIECES)),
            dma((4, SCATTER_PIECES)), dma((4, 2, SCATTER_PIECES)), dma((15,)), dma((16,)), dma((15,)), dma((16,)),
        ],
        compiler_params=pltpu.CompilerParams(vmem_limit_bytes=LIMIT, collective_id=2, has_side_effects=True),
        name="scatter_gradients",
    )(count, info, tiles, pairs, wsum, src_scale)


def put_kernel(*refs):
    count = len(refs) // 2
    ins, outs, sems = refs[:count], refs[count : 2 * count], refs[-1]
    copies = [pltpu.make_async_copy(ins[k], outs[k], sems.at[k]) for k in range(count)]
    for copy in copies:
        copy.start()
    for copy in copies:
        copy.wait()


def put_out(*arrays):
    return pl.pallas_call(
        put_kernel,
        in_specs=[VMEM_SPEC] * len(arrays),
        out_specs=[pl.BlockSpec(memory_space=pltpu.HBM)] * len(arrays),
        out_shape=[jax.ShapeDtypeStruct(array.shape, array.dtype) for array in arrays],
        scratch_shapes=[pltpu.SemaphoreType.DMA((len(arrays),))],
        compiler_params=pltpu.CompilerParams(vmem_limit_bytes=LIMIT),
        name="put_out",
    )(*arrays)


def local(features, weight, bias_vector, out_grad, adj_tiles, tile_slots, tile_counts):
    tiles, pairs, src_scale, dst_scale, forward_info, backward_info = gather_features(
        features, adj_tiles[0, 0], tile_slots[0], tile_counts
    )
    activated, grad_pairs, wsum = dense_layer(
        tile_counts, forward_info, tiles, pairs, weight, bias_vector, out_grad, dst_scale
    )
    feature_grad, weight_grad, bias_grad = scatter_gradients(
        tile_counts, backward_info, tiles, grad_pairs, wsum, src_scale
    )
    activated, feature_grad, weight_grad, bias_grad = put_out(activated, feature_grad, weight_grad, bias_grad)
    return activated, feature_grad, weight_grad, bias_grad.reshape(TILE)


def solution(mesh):
    return jax.shard_map(
        local,
        mesh=mesh,
        in_specs=(
            P(("col", "row"), None),
            P(),
            P(),
            P(("row", "col"), None),
            P("row", "col", None, None, None),
            P("row", "col", None),
            P("row", "col"),
        ),
        out_specs=(P(("row", "col"), None), P(("col", "row"), None), P(), P()),
        check_vma=False,
    )
```

```python
import functools

import jax
import jax.numpy as jnp
from jax import lax
from jax.experimental import pallas as pl
from jax.experimental.pallas import tpu as pltpu
from jax.sharding import PartitionSpec as P

TILE = 128
MESH = pl.DeviceIdType.MESH
F32 = jnp.float32
BF16 = jnp.bfloat16
HIGHEST = lax.Precision.HIGHEST
VMEM_SPEC = pl.BlockSpec(memory_space=pltpu.VMEM)
CHUNK = 8
LIMIT = 24 << 20
GATHER_PIECES = 2
GATHER_ROWS = ((0, 96), (96, 96), (192, 64))
LAYER_PIECES = 2
SCATTER_PIECES = 2


def block_of(pieces):
    return (pieces, 2 * TILE // pieces, TILE)


def by_way(pieces):
    return [(piece % 2, piece) for piece in range(pieces)] + [(piece % 2, piece + 1 - 2 * (piece % 2)) for piece in range(pieces)]


def piece_columns(scale_ref, first, pieces):
    columns = [to_column(scale_ref[pl.ds(first + half, 1), :]) for half in (0, 1)]
    each = pieces // 2
    rows = TILE // each
    return [columns[k // each][k % each * rows : (k % each + 1) * rows] for k in range(pieces)]
NT = (((1,), (1,)), ((), ()))
NN = (((1,), (0,)), ((), ()))
TN = (((0,), (0,)), ((), ()))


def remote(src, dst, send_sem, recv_sem, **where):
    return pltpu.make_async_remote_copy(
        src_ref=src,
        dst_ref=dst,
        send_sem=send_sem,
        recv_sem=recv_sem,
        device_id=where,
        device_id_type=MESH,
    )


def xor_peer(index, bit):
    return index + bit - 2 * bit * lax.rem(lax.div(index, bit), 2)


def greet(rows, cols):
    barrier = pltpu.get_barrier_semaphore()
    for peer in rows:
        pl.semaphore_signal(barrier, inc=1, device_id={"row": peer}, device_id_type=MESH)
    for peer in cols:
        pl.semaphore_signal(barrier, inc=1, device_id={"col": peer}, device_id_type=MESH)
    return lambda: pl.semaphore_wait(barrier, len(rows) + len(cols))


def to_column(row_vector):
    spread = jnp.broadcast_to(row_vector, (TILE, TILE))
    diagonal = lax.broadcasted_iota(jnp.int32, (TILE, TILE), 0) == lax.broadcasted_iota(
        jnp.int32, (TILE, TILE), 1
    )
    return jnp.sum(jnp.where(diagonal, spread, 0.0), axis=1, keepdims=True)


def split_pair(value):
    high = value.astype(BF16)
    low = (value - high.astype(F32)).astype(BF16)
    return jnp.concatenate([high, low], axis=1)


def put_pair(pair_ref, block, piece, pieces, value):
    each = pieces // 2
    rows = TILE // each
    here = slice(piece % each * rows, (piece % each + 1) * rows)
    pair_ref[2 * block + piece // each, here, :] = split_pair(value)


def sort_table(slots, live, by_row):
    tile_row = jnp.floor(slots * (1.0 / 32.0))
    tile_col = slots - 32.0 * tile_row
    lane = lax.broadcasted_iota(jnp.int32, (1, TILE), 1).astype(F32)
    key = jnp.where(live, tile_row * 32.0 + tile_col if by_row else tile_col * 32.0 + tile_row, 2048.0 + lane)
    key_column = to_column(key)
    rank = jnp.sum(jnp.where(key < key_column, 1.0, 0.0), axis=1, keepdims=True)
    place = rank == lax.broadcasted_iota(jnp.int32, (TILE, TILE), 1).astype(F32)
    number = lax.broadcasted_iota(jnp.int32, (TILE, 1), 0).astype(F32)

    def moved(column):
        return jnp.sum(jnp.where(place, column, 0.0), axis=0, keepdims=True).astype(jnp.int32)

    ends = (to_column(tile_row), to_column(tile_col))
    if not by_row:
        ends = ends[::-1]
    live_column = to_column(jnp.where(live, 1.0, 0.0))
    target = lax.broadcasted_iota(jnp.int32, (TILE, TILE), 1).astype(F32)

    def counted(which):
        return jnp.sum(jnp.where(which, live_column, 0.0), axis=0, keepdims=True).astype(jnp.int32)

    return moved(number), moved(ends[0]), moved(ends[1]), counted(ends[0] < target), counted(ends[0] <= target)


def block_product(dims, count_ref, info_ref, tiles_ref, pair_ref, sums_ref, first, last, total):
    unroll = 8
    count = count_ref[0, 0]

    def body(step, total):
        for u in range(unroll):
            k = step * unroll + u
            at = jnp.clip(count - 1, 0, k)
            number = jnp.clip(info_ref[0, at], 0, tiles_ref.shape[0] - 1)
            source = jnp.clip(info_ref[2, at], 0, pair_ref.shape[0] - 1)
            both = lax.dot_general(tiles_ref[number], pair_ref[source], dims, preferred_element_type=F32)
            goes_on = (k > 0) & (info_ref[1, jnp.maximum(at - 1, 0)] == info_ref[1, at])
            total = both[:, :TILE] + both[:, TILE:] + jnp.where(goes_on, total, 0.0)
            sums_ref[k] = total
        return total

    return lax.fori_loop(first, last, body, total)


def take_block(info_ref, sums_ref, part_ref, block):
    rows = part_ref.shape[2]
    each = TILE // rows
    for half in (0, 1):
        first, end = info_ref[3, 2 * block + half], info_ref[4, 2 * block + half]
        tile = jnp.where(end > first, sums_ref[jnp.clip(end - 1, 0, sums_ref.shape[0] - 1)], 0.0)
        for k in range(each):
            part_ref[block, half * each + k] = tile[k * rows : (k + 1) * rows]


def split_rows(value, order):
    high = value.astype(BF16)
    low = (value - high.astype(F32)).astype(BF16)
    return jnp.concatenate([(high, low)[k] for k in order], axis=0)


def split_columns(value):
    high = value.astype(BF16)
    low = (value - high.astype(F32)).astype(BF16)
    return jnp.concatenate([high, low, high], axis=1)


OUTWARD = ((0, 1, 2, 3), (1, 0, 2, 3), (2, 1, 3, 0), (3, 2, 1, 0))
INWARD = tuple(order[::-1] for order in OUTWARD)


def in_order(orders, place, z):
    low, high = lax.rem(z, 2), lax.div(z, 2)
    v = [orders[k][place] for k in range(4)]
    return v[0] + (v[1] - v[0]) * low + (v[2] - v[0]) * high + (v[3] - v[2] - v[1] + v[0]) * low * high


def gather_kernel(
    count_ref, slots_ref, feat_ref, adj_ref,
    tiles_ref, pair_ref, src_scale_ref, dst_scale_ref, forward_info_ref, backward_info_ref,
    adj_got, row_sums, col_sums, parts, held, slots_got, deg_sent, deg_got,
    feat_sem, adj_sem, recv_sem, z_sem, y_sem, relay_sem, across_sem, along_sem, deg_send_sem, deg_recv_sem,
):
    chunks = adj_ref.shape[0] // CHUNK
    row, col = lax.axis_index("row"), lax.axis_index("col")
    y, z = lax.div(row, 4), lax.rem(row, 4)
    y_up, y_down, y_far = lax.rem(y + 1, 4), lax.rem(y + 3, 4), lax.rem(y + 2, 4)
    wait_for_all = greet(
        [lax.rem(y + d, 4) * 4 + z for d in (1, 2, 3)] + [y * 4 + lax.rem(z + d, 4) for d in (1, 2, 3)],
        [xor_peer(col, bit) for bit in (1, 2, 4, 8)],
    )

    def adj_copy(chunk):
        here = pl.ds(pl.multiple_of(chunk * CHUNK, CHUNK), CHUNK)
        return pltpu.make_async_copy(adj_ref.at[here], adj_got.at[here], adj_sem.at[chunk])

    feat_copy = pltpu.make_async_copy(feat_ref, held.at[row], feat_sem.at[0])
    feat_copy.start()
    slots_copy = pltpu.make_async_copy(slots_ref, slots_got, feat_sem.at[1])
    slots_copy.start()
    for chunk in range(chunks):
        adj_copy(chunk).start()

    ones = jnp.ones((TILE, TILE), F32).astype(BF16)
    diagonal = lax.broadcasted_iota(jnp.int32, (TILE, TILE), 0) == lax.broadcasted_iota(
        jnp.int32, (TILE, TILE), 1
    )

    def degree_chunks(first, last):
        def body(chunk, carry):
            adj_copy(chunk).wait()
            for k in range(CHUNK):
                slot = chunk * CHUNK + k
                tile = adj_got[slot].astype(F32)
                narrow = tile.astype(BF16)
                tiles_ref[slot] = narrow
                col_sums[pl.ds(slot, 1), :] = jnp.sum(tile, axis=0, keepdims=True)
                sums = jnp.dot(narrow, ones, preferred_element_type=F32)
                row_sums[pl.ds(slot, 1), :] = jnp.sum(jnp.where(diagonal, sums, 0.0), axis=0, keepdims=True)
            return carry

        lax.fori_loop(first, last, body, 0)

    slots_copy.wait()
    slots = slots_got[...].astype(F32)
    live = lax.broadcasted_iota(jnp.int32, (1, TILE), 1) < count_ref[0, 0]

    def degree_parts():
        tile_row = jnp.floor(slots * (1.0 / 32.0))
        tile_col = slots - 32.0 * tile_row
        tile_number = lax.broadcasted_iota(jnp.int32, (32, TILE), 0).astype(F32)
        row_select = jnp.where(live & (tile_row == tile_number), 1.0, 0.0).astype(BF16)
        col_select = jnp.where(live & (tile_col == tile_number), 1.0, 0.0).astype(BF16)
        parts[0] = jnp.dot(col_select, col_sums[...].astype(BF16), preferred_element_type=F32)
        parts[1] = jnp.dot(row_select, row_sums[...].astype(BF16), preferred_element_type=F32)

    def part_of(block, piece):
        return held.at[block, pl.ds(*GATHER_ROWS[piece])]

    def z_copy(z_from, way, piece):
        block = y * 4 + z_from
        return remote(
            part_of(block, piece), part_of(block, piece),
            z_sem.at[z_from, way, piece], recv_sem.at[block, piece],
            row=y * 4 + lax.rem(z + (1 if way == 0 else 3), 4),
        )

    def y_copy(z_from, way, piece):
        block = y * 4 + z_from
        return remote(
            part_of(block, piece), part_of(block, piece),
            y_sem.at[z_from, way, piece], recv_sem.at[block, piece],
            row=(y_up, y_down)[way] * 4 + z,
        )

    def relay_copy(z_from, piece):
        way = piece % 2
        block = (y_down, y_up)[way] * 4 + z_from
        return remote(
            part_of(block, piece), part_of(block, piece),
            relay_sem.at[z_from, piece], recv_sem.at[block, piece],
            row=(y_up, y_down)[way] * 4 + z,
        )

    def arrived(block, piece):
        remote(
            part_of(block, piece), part_of(block, piece), relay_sem.at[0, piece], recv_sem.at[block, piece],
            row=y_up * 4 + z,
        ).wait_recv()

    def on_line(place, pieces, action):
        z_from = in_order(OUTWARD, place, z)
        for way in (0, 1):
            goes = z < 3 if way == 0 else z > 0
            if place:
                goes = goes & (z_from < z if way == 0 else z_from > z)

            @pl.when(goes)
            def _():
                for piece in pieces:
                    action(z_copy(z_from, way, piece))

    def column_step(place):
        z_from = in_order(OUTWARD, place, z)
        if place:
            for piece in range(GATHER_PIECES):
                arrived(y * 4 + z_from, piece)
        on_line(place, range(GATHER_PIECES), lambda copy: copy.start())
        for way, piece in by_way(GATHER_PIECES):
            y_copy(z_from, way, piece).start()

    def across_copy(place):
        return remote(
            part_of(row, 2), part_of(row, 2), across_sem.at[place], recv_sem.at[row, 2],
            row=(y_up, y_down, y_far)[place] * 4 + z,
        )

    def along_copy(turn, z_from, way):
        block = lax.rem(y + turn, 4) * 4 + z_from
        return remote(
            part_of(block, 2), part_of(block, 2), along_sem.at[turn, z_from, way], recv_sem.at[block, 2],
            row=y * 4 + lax.rem(z + (1 if way == 0 else 3), 4),
        )

    def along_step(place, turns, action, wait=True):
        z_from = in_order(OUTWARD, place, z)
        for turn in turns:
            if wait and (place or turn):
                arrived(lax.rem(y + turn, 4) * 4 + z_from, 2)
            for way in (0, 1):
                goes = z < 3 if way == 0 else z > 0
                if place:
                    goes = goes & (z_from < z if way == 0 else z_from > z)
                pl.when(goes)(lambda: action(along_copy(turn, z_from, way)))

    def start(copy):
        copy.start()

    def wait_send(copy):
        copy.wait_send()

    def relay_step(place):
        z_from = in_order(OUTWARD, place, z)
        for piece in range(GATHER_PIECES):
            arrived((y_down, y_up)[piece % 2] * 4 + z_from, piece)
            relay_copy(z_from, piece).start()

    def degree_source(which, step):
        return parts.at[which] if step == 0 else deg_sent.at[which, step - 1]

    def degree_copy(which, step):
        where = {("row", "col")[which]: xor_peer((row, col)[which], 1 << step)}
        return remote(
            degree_source(which, step), deg_got.at[which, step],
            deg_send_sem.at[which, step], deg_recv_sem.at[which, step], **where
        )

    def degree_step(step):
        for which in (0, 1):
            degree_copy(which, step).wait_recv()
            deg_sent[which, step] = degree_source(which, step)[...] + deg_got[which, step]
            if step < 3:
                degree_copy(which, step + 1).start()

    feat_copy.wait()
    wait_for_all()
    for place in range(3):
        across_copy(place).start()
    column_step(0)
    along_step(0, (0,), start)
    degree_chunks(0, chunks // 2)
    along_step(0, (1, 3, 2), start)
    relay_step(0)
    column_step(1)
    degree_chunks(chunks // 2, chunks)
    degree_parts()
    for which in (0, 1):
        degree_copy(which, 0).start()
    along_step(1, range(4), start)
    relay_step(1)
    column_step(2)
    degree_step(0)
    along_step(2, range(4), start)
    relay_step(2)
    degree_step(1)
    column_step(3)
    degree_step(2)
    for info_ref, by_row in ((forward_info_ref, True), (backward_info_ref, False)):
        for place, line in enumerate(sort_table(slots, live, by_row)):
            info_ref[place : place + 1, :] = line
    relay_step(3)
    along_step(3, range(4), start)
    degree_step(3)

    src_scale_ref[...] = lax.rsqrt(1.0 + deg_sent[0, 3])
    dst_scale_ref[...] = lax.rsqrt(1.0 + deg_sent[1, 3])

    def settle(block):
        for half, scale in enumerate(piece_columns(src_scale_ref, 2 * block, 2)):
            put_pair(pair_ref, block, half, 2, held[block, half * TILE : half * TILE + TILE, :] * scale)

    for place in range(4):
        settle(y * 4 + in_order(OUTWARD, place, z))
    for place in range(4):
        z_from = in_order(OUTWARD, place, z)
        for way in (0, 1):
            block = (y_down, y_up)[way] * 4 + z_from
            for piece in range(1 - way, GATHER_PIECES, 2):
                arrived(block, piece)
            settle(block)
    for place in range(4):
        z_from = in_order(OUTWARD, place, z)
        for piece in range(GATHER_PIECES):
            arrived(y_far * 4 + z_from, piece)
        settle(y_far * 4 + z_from)
    for place in range(4):
        z_from = in_order(OUTWARD, place, z)
        for piece in range(GATHER_PIECES):
            for way in (0, 1):
                y_copy(z_from, way, piece).wait_send()
            relay_copy(z_from, piece).wait_send()
        on_line(place, range(GATHER_PIECES), lambda copy: copy.wait_send())
        along_step(place, range(4), wait_send, wait=False)
    for place in range(3):
        across_copy(place).wait_send()
    for which in (0, 1):
        for step in range(4):
            degree_copy(which, step).wait_send()


def gather_features(features, adj_tiles, slots, count):
    dma = pltpu.SemaphoreType.DMA
    slot_total = adj_tiles.shape[0]
    return pl.pallas_call(
        gather_kernel,
        in_specs=[
            pl.BlockSpec(memory_space=pltpu.SMEM),
            pl.BlockSpec(memory_space=pltpu.HBM),
            pl.BlockSpec(memory_space=pltpu.HBM),
            pl.BlockSpec(memory_space=pltpu.HBM),
        ],
        out_specs=[VMEM_SPEC] * 6,
        out_shape=[
            jax.ShapeDtypeStruct((slot_total, TILE, TILE), BF16),
            jax.ShapeDtypeStruct((32, TILE, 2 * TILE), BF16),
            jax.ShapeDtypeStruct((32, TILE), F32),
            jax.ShapeDtypeStruct((32, TILE), F32),
            jax.ShapeDtypeStruct((5, TILE), jnp.int32),
            jax.ShapeDtypeStruct((5, TILE), jnp.int32),
        ],
        scratch_shapes=[
            pltpu.VMEM((slot_total, TILE, TILE), jnp.int32),
            pltpu.VMEM((slot_total, TILE), F32),
            pltpu.VMEM((slot_total, TILE), F32),
            pltpu.VMEM((2, 32, TILE), F32),
            pltpu.VMEM((16, 2 * TILE, TILE), F32),
            pltpu.VMEM((1, TILE), jnp.int32),
            pltpu.VMEM((2, 4, 32, TILE), F32),
            pltpu.VMEM((2, 4, 32, TILE), F32),
            dma((2,)),
            dma((slot_total // CHUNK,)),
            dma((16, 3)),
            dma((4, 2, GATHER_PIECES)),
            dma((4, 2, GATHER_PIECES)),
            dma((4, GATHER_PIECES)),
            dma((3,)),
            dma((4, 4, 2)),
            dma((2, 4)),
            dma((2, 4)),
        ],
        compiler_params=pltpu.CompilerParams(vmem_limit_bytes=LIMIT, collective_id=0, has_side_effects=True),
        name="gather_features",
    )(
        count,
        pltpu.with_memory_space_constraint(slots, pltpu.HBM),
        pltpu.with_memory_space_constraint(features, pltpu.HBM),
        pltpu.with_memory_space_constraint(adj_tiles, pltpu.HBM),
    )


SLICE = (16, TILE)


def layer_kernel(
    count_ref, info_ref, tiles_ref, source_ref, w_ref, b_ref, grad_ref, scale_ref, act_ref, pair_ref, wsum_ref,
    sums, part_ref, w_fore, w_back, sib_got, ring, from_left, from_right, z_sent, z_got, held, aggs, grads, wgrad, w_got,
    sib_ssem, sib_rsem, far_ssem, far_rsem, near_ssem, near_rsem, z_ssem, z_rsem,
    recv_sem, zg_sem, xg_sem, relay_sem, sg_sem, w_ssem, w_rsem,
):
    col = lax.axis_index("col")
    x, zh, core = lax.div(col, 4), lax.rem(lax.div(col, 2), 2), lax.rem(col, 2)
    x_up, x_down, x_far = lax.rem(x + 1, 4), lax.rem(x + 3, 4), lax.rem(x + 2, 4)
    sibling = col + 1 - 2 * core
    z_peer = col + 2 - 4 * zh
    up, down = x_up * 4 + zh * 2 + core, x_down * 4 + zh * 2 + core
    wait_for_all = greet([], [lax.rem(col + d, 16) for d in range(1, 16)])
    block_product(
        NN, count_ref, info_ref, tiles_ref, source_ref, sums, 0, tiles_ref.shape[0] // 8, jnp.zeros((TILE, TILE), F32)
    )
    w_fore[...] = split_rows(w_ref[...], (0, 0, 1))
    w_back[...] = split_rows(jnp.transpose(w_ref[...]), (0, 0, 1))
    first, rest = (0, 1), range(2, LAYER_PIECES)
    after = [(piece % 2, piece + 1 - 2 * (piece % 2)) for piece in rest]

    def sib_copy(place, which):
        target = (x_far, x_up, x_down, x)[place]
        half_z = 1 - zh if which == 0 else zh
        return remote(
            part_ref.at[target * 4 + half_z * 2 + 1 - core], sib_got.at[place, which],
            sib_ssem.at[place, which], sib_rsem.at[place, which], col=sibling,
        )

    def far_copy(which, piece):
        return remote(
            sib_got.at[0, which, piece], ring.at[which, piece],
            far_ssem.at[which, piece], far_rsem.at[which, piece], col=(up, down)[piece % 2],
        )

    def near_copy(which, way, piece):
        return remote(
            sib_got.at[1 + way, which, piece], (from_left, from_right)[way].at[which, piece],
            near_ssem.at[which, way, piece], near_rsem.at[which, way, piece], col=(up, down)[way],
        )

    def z_copy(piece):
        return remote(z_sent.at[piece], z_got.at[piece], z_ssem.at[piece], z_rsem.at[piece], col=z_peer)

    def join(place, which):
        target = (x_far, x_up, x_down, x)[place]
        half_z = 1 - zh if which == 0 else zh
        sib_copy(place, which).wait_recv()
        sib_got[place, which] += part_ref[target * 4 + half_z * 2 + core]

    def open_ring(which):
        join(0, which)
        for piece in range(LAYER_PIECES):
            far_copy(which, piece).start()
        for way in (0, 1):
            join(1 + way, which)
            near_copy(which, way, 1 - way).start()
        join(3, which)

    def relay_ring(which, pieces):
        for piece in pieces:
            way = piece % 2
            far_copy(which, piece).wait_recv()
            sib_got[1 + way, which, piece] += ring[which, piece]
            near_copy(which, way, piece).start()

    def rest_ring(which):
        for way, piece in after:
            near_copy(which, way, piece).start()

    def ring_total(which, piece):
        for way in (0, 1):
            near_copy(which, way, piece).wait_recv()
        return sib_got[3, which, piece] + from_left[which, piece] + from_right[which, piece]

    def send_over(pieces):
        for piece in pieces:
            z_sent[piece] = ring_total(0, piece)
            z_copy(piece).start()

    wait_for_all()
    for which in (0, 1):
        for place in range(4):
            target = (x_far, x_up, x_down, x)[place] * 4 + (1 - zh if which == 0 else zh) * 2
            take_block(info_ref, sums, part_ref, target + 1 - core)
            sib_copy(place, which).start()
            take_block(info_ref, sums, part_ref, target + core)
    open_ring(0)
    relay_ring(0, first)
    rest_ring(0)
    relay_ring(0, rest)
    open_ring(1)
    send_over(first)
    relay_ring(1, first)
    rest_ring(1)
    send_over(rest)
    relay_ring(1, rest)

    def spread_z(piece):
        return remote(
            held.at[col, piece], held.at[col, piece], zg_sem.at[piece], recv_sem.at[col, piece], col=z_peer
        )

    def spread_x(which, way, piece):
        half_z = zh if which == 0 else 1 - zh
        block = x * 4 + half_z * 2 + core
        return remote(
            held.at[block, piece], held.at[block, piece], xg_sem.at[which, way, piece], recv_sem.at[block, piece],
            col=(up, down)[way],
        )

    def relay_x(which, piece):
        half_z = zh if which == 0 else 1 - zh
        way = piece % 2
        block = (x_down, x_up)[way] * 4 + half_z * 2 + core
        return remote(
            held.at[block, piece], held.at[block, piece], relay_sem.at[which, piece], recv_sem.at[block, piece],
            col=(up, down)[way],
        )

    def spread_sib(place, which, piece):
        target = (x, x_up, x_down, x_far)[place]
        half_z = zh if which == 0 else 1 - zh
        block = target * 4 + half_z * 2 + core
        return remote(
            held.at[block, piece], held.at[block, piece], sg_sem.at[place, which, piece], recv_sem.at[block, piece],
            col=sibling,
        )

    def arrived(block, piece):
        remote(
            held.at[block, piece], held.at[block, piece], zg_sem.at[piece], recv_sem.at[block, piece], col=sibling
        ).wait_recv()

    def spread(which, piece):
        way = piece % 2
        spread_x(which, way, piece).start()
        spread_x(which, 1 - way, piece).start()
        spread_sib(0, which, piece).start()

    def settle(block, piece):
        put_pair(pair_ref, block, piece, LAYER_PIECES, held[block, piece])

    for piece, scale in enumerate(piece_columns(scale_ref, 2 * col, LAYER_PIECES)):
        here = slice(piece * part_ref.shape[2], (piece + 1) * part_ref.shape[2])
        own = ring_total(1, piece)
        z_copy(piece).wait_recv()
        aggregated = (own + z_got[piece]) * scale
        preact = jnp.dot(split_columns(aggregated), w_fore[...], preferred_element_type=F32) + b_ref[...]
        logistic = 1.0 / (1.0 + jnp.exp(-preact))
        pre_grad = grad_ref[here, :] * logistic * (1.0 + preact * (1.0 - logistic))
        held[col, piece] = scale * jnp.dot(split_columns(pre_grad), w_back[...], preferred_element_type=F32)
        spread_z(piece).start()
        spread(0, piece)
        act_ref[here, :] = preact * logistic
        aggs[here, :] = aggregated
        grads[here, :] = pre_grad

    weight_part = lax.dot_general(
        split_rows(aggs[...], (0, 1, 0)), split_rows(grads[...], (0, 0, 1)), TN, preferred_element_type=F32
    )
    bias_part = jnp.broadcast_to(jnp.sum(grads[...], axis=0, keepdims=True), (8, TILE))
    for part in range(16):
        wgrad[part, 0:8, :] = weight_part[part * 8 : part * 8 + 8]
        wgrad[part, 8:16, :] = bias_part

    def w_copy(distance):
        peer = lax.rem(col + distance, 16)
        return remote(
            wgrad.at[peer], w_got.at[distance - 1], w_ssem.at[distance - 1], w_rsem.at[distance - 1], col=peer
        )

    for distance in range(1, 16):
        w_copy(distance).start()

    def relay(which, pieces):
        half_z = zh if which == 0 else 1 - zh
        for piece in pieces:
            way = piece % 2
            arrived((x_down, x_up)[way] * 4 + half_z * 2 + core, piece)
            relay_x(which, piece).start()
            spread_sib((2, 1)[way], which, piece).start()

    def near_rest(which):
        half_z = zh if which == 0 else 1 - zh
        for piece in range(LAYER_PIECES):
            way = piece % 2
            arrived((x_up, x_down)[way] * 4 + half_z * 2 + core, piece)
            spread_sib((1, 2)[way], which, piece).start()

    def far_rest(which):
        half_z = zh if which == 0 else 1 - zh
        for piece in range(LAYER_PIECES):
            arrived(x_far * 4 + half_z * 2 + core, piece)
            spread_sib(3, which, piece).start()

    other = x * 4 + (1 - zh) * 2 + core

    def take_over(piece):
        arrived(other, piece)
        spread(1, piece)

    relay(0, range(LAYER_PIECES))
    near_rest(0)
    for piece in range(LAYER_PIECES):
        take_over(piece)
        if piece == 1:
            far_rest(0)
        if piece >= 2:
            relay(1, (piece - 2,))
    for piece in range(max(LAYER_PIECES - 2, 0), LAYER_PIECES - 1):
        relay(1, (piece,))
    for side in (x, x_up):
        for piece in range(LAYER_PIECES):
            settle(side * 4 + zh * 2 + core, piece)
    relay(1, (LAYER_PIECES - 1,))
    for side in (x_down, x_far):
        for piece in range(LAYER_PIECES):
            settle(side * 4 + zh * 2 + core, piece)
    near_rest(1)
    for side in (x, x_up, x_down, x_far):
        for piece in range(LAYER_PIECES):
            block = side * 4 + zh * 2 + 1 - core
            arrived(block, piece)
            settle(block, piece)
    far_rest(1)
    for side in (x, x_up, x_down, x_far):
        for piece in range(LAYER_PIECES):
            settle(side * 4 + (1 - zh) * 2 + core, piece)
            block = side * 4 + (1 - zh) * 2 + 1 - core
            arrived(block, piece)
            settle(block, piece)

    wsum = wgrad[col]
    for distance in range(1, 16):
        w_copy(distance).wait_recv()
        wsum += w_got[distance - 1]
    wsum_ref[...] = wsum
    for which in (0, 1):
        for place in range(4):
            sib_copy(place, which).wait_send()
            for piece in range(LAYER_PIECES):
                spread_sib(place, which, piece).wait_send()
        for piece in range(LAYER_PIECES):
            far_copy(which, piece).wait_send()
            relay_x(which, piece).wait_send()
            for way in (0, 1):
                near_copy(which, way, piece).wait_send()
                spread_x(which, way, piece).wait_send()
    for piece in range(LAYER_PIECES):
        z_copy(piece).wait_send()
        spread_z(piece).wait_send()
    for distance in range(1, 16):
        w_copy(distance).wait_send()


def dense_layer(count, info, tiles, pairs, weight, bias_vector, out_grad, dst_scale):
    dma = pltpu.SemaphoreType.DMA
    block = block_of(LAYER_PIECES)
    return pl.pallas_call(
        layer_kernel,
        in_specs=[pl.BlockSpec(memory_space=pltpu.SMEM)] * 2 + [VMEM_SPEC] * 6,
        out_specs=[VMEM_SPEC] * 3,
        out_shape=[
            jax.ShapeDtypeStruct((2 * TILE, TILE), F32),
            jax.ShapeDtypeStruct((32, TILE, 2 * TILE), BF16),
            jax.ShapeDtypeStruct(SLICE, F32),
        ],
        scratch_shapes=[
            pltpu.VMEM(tiles.shape, F32),
            pltpu.VMEM((16,) + block, F32),
            pltpu.VMEM((3 * TILE, TILE), BF16),
            pltpu.VMEM((3 * TILE, TILE), BF16),
            pltpu.VMEM((4, 2) + block, F32),
            pltpu.VMEM((2,) + block, F32),
            pltpu.VMEM((2,) + block, F32),
            pltpu.VMEM((2,) + block, F32),
            pltpu.VMEM(block, F32),
            pltpu.VMEM(block, F32),
            pltpu.VMEM((16,) + block, F32),
            pltpu.VMEM((2 * TILE, TILE), F32),
            pltpu.VMEM((2 * TILE, TILE), F32),
            pltpu.VMEM((16,) + SLICE, F32),
            pltpu.VMEM((15,) + SLICE, F32),
            dma((4, 2)), dma((4, 2)), dma((2, LAYER_PIECES)), dma((2, LAYER_PIECES)),
            dma((2, 2, LAYER_PIECES)), dma((2, 2, LAYER_PIECES)), dma((LAYER_PIECES,)), dma((LAYER_PIECES,)),
            dma((16, LAYER_PIECES)), dma((LAYER_PIECES,)), dma((2, 2, LAYER_PIECES)), dma((2, LAYER_PIECES)), dma((4, 2, LAYER_PIECES)),
            dma((15,)), dma((15,)),
        ],
        compiler_params=pltpu.CompilerParams(vmem_limit_bytes=LIMIT, collective_id=1, has_side_effects=True),
        name="dense_layer",
    )(count, info, tiles, pairs, weight, bias_vector.reshape(1, TILE), out_grad, dst_scale)


def scatter_kernel(
    count_ref, info_ref, tiles_ref, source_ref, wsum_ref, scale_ref, grad_ref, wgrad_ref, bgrad_ref,
    sums, part_ref, staged, ring, from_down, from_up, total, line_up, line_down, w_got, w_all,
    far_ssem, far_rsem, near_ssem, near_rsem, line_ssem, line_rsem, w_ssem, w_rsem, all_ssem, all_rsem,
):
    row, col = lax.axis_index("row"), lax.axis_index("col")
    y, z = lax.div(row, 4), lax.rem(row, 4)
    y_up, y_down, y_far = lax.rem(y + 1, 4), lax.rem(y + 3, 4), lax.rem(y + 2, 4)
    wait_for_all = greet(
        [lax.rem(row + d, 16) for d in range(1, 16)], [lax.rem(col + d, 16) for d in range(1, 16)]
    )
    up, down = y_up * 4 + z, y_down * 4 + z

    def far_copy(zb, piece):
        return remote(
            part_ref.at[y_far * 4 + zb, piece], ring.at[zb, piece],
            far_ssem.at[zb, piece], far_rsem.at[zb, piece], row=(up, down)[piece % 2],
        )

    def near_copy(zb, way, piece):
        block = (y_up, y_down)[way] * 4 + zb
        source = staged.at[zb, piece] if piece % 2 == way else part_ref.at[block, piece]
        return remote(
            source, (from_down, from_up)[way].at[zb, piece],
            near_ssem.at[zb, way, piece], near_rsem.at[zb, way, piece], row=(up, down)[way],
        )

    def line_copy(zb, way, piece):
        return remote(
            total.at[zb, piece], (line_up, line_down)[way].at[zb, piece],
            line_ssem.at[zb, piece], line_rsem.at[zb, way, piece],
            row=y * 4 + lax.rem(z + (1 if way == 0 else 3), 4),
        )

    def w_copy(distance):
        return remote(
            wsum_ref, w_got.at[row], w_ssem.at[distance - 1], w_rsem.at[row], row=lax.rem(row + distance, 16)
        )

    def w_arrived(distance):
        sender = lax.rem(row + distance, 16)
        remote(wsum_ref, w_got.at[sender], w_ssem.at[distance - 1], w_rsem.at[sender], row=sender).wait_recv()

    def all_copy(distance):
        return remote(
            w_all.at[col], w_all.at[col], all_ssem.at[distance - 1], all_rsem.at[col], col=lax.rem(col + distance, 16)
        )

    def all_arrived(distance):
        sender = lax.rem(col + distance, 16)
        remote(
            w_all.at[sender], w_all.at[sender], all_ssem.at[distance - 1], all_rsem.at[sender], col=sender
        ).wait_recv()

    def w_total():
        for distance in range(1, 16):
            w_arrived(distance)
        whole = w_got[0]
        for sender in range(1, 16):
            whole += w_got[sender]
        w_all[col] = whole
        for distance in range(1, 16):
            all_copy(distance).start()

    zbs = [in_order(INWARD, place, z) for place in range(4)]

    def far_step(place):
        for piece in range(SCATTER_PIECES):
            far_copy(zbs[place], piece).start()

    def near_step(place, pieces):
        for way in (0, 1):
            for piece in pieces:
                if piece % 2 != way:
                    near_copy(zbs[place], way, piece).start()

    def relay_step(place, pieces):
        zb = zbs[place]
        for piece in pieces:
            way = piece % 2
            far_copy(zb, piece).wait_recv()
            staged[zb, piece] = part_ref[(y_up, y_down)[way] * 4 + zb, piece] + ring[zb, piece]
            near_copy(zb, way, piece).start()

    def line_ways(place):
        zb = zbs[place]
        if place == 3:
            return ((0, z > 0, None), (1, z < 3, None))
        return ((0, (zb > z) & (z > 0), zb > z), (1, (zb < z) & (z < 3), zb < z))

    def close_step(place):
        zb = zbs[place]
        for piece in range(SCATTER_PIECES):
            for way in (0, 1):
                near_copy(zb, way, piece).wait_recv()
            total[zb, piece] = part_ref[y * 4 + zb, piece] + from_down[zb, piece] + from_up[zb, piece]
            for way, comes, goes in line_ways(place):

                @pl.when(comes)
                def _():
                    line_copy(zb, way, piece).wait_recv()
                    total[zb, piece] += (line_up, line_down)[way][zb, piece]

                if goes is not None:
                    pl.when(goes)(lambda: line_copy(zb, way, piece).start())

    def send_step(place):
        zb = zbs[place]
        for piece in range(SCATTER_PIECES):
            far_copy(zb, piece).wait_send()
            for way in (0, 1):
                near_copy(zb, way, piece).wait_send()
        for way, _, goes in line_ways(place):
            for piece in range(SCATTER_PIECES):
                if goes is not None:
                    pl.when(goes)(lambda: line_copy(zb, way, piece).wait_send())

    def product_part(first, last, so_far):
        return block_product(TN, count_ref, info_ref, tiles_ref, source_ref, sums, first, last, so_far)

    groups = tiles_ref.shape[0] // 8
    so_far = product_part(0, groups // 2, jnp.zeros((TILE, TILE), F32))
    wait_for_all()
    for distance in range(1, 16):
        w_copy(distance).start()
    w_got[row] = wsum_ref[...]
    product_part(groups // 2, groups, so_far)
    for place in range(4):
        take_block(info_ref, sums, part_ref, y_far * 4 + zbs[place])
        if place == 0:
            far_step(0)
        for side in (y_up, y_down):
            take_block(info_ref, sums, part_ref, side * 4 + zbs[place])
        if place == 0:
            near_step(0, range(SCATTER_PIECES))
        if place == 1:
            far_step(1)
        take_block(info_ref, sums, part_ref, y * 4 + zbs[place])
    for place in range(4):
        relay_step(place, range(SCATTER_PIECES))
        if place < 3:
            near_step(place + 1, range(SCATTER_PIECES))
        if place < 2:
            far_step(place + 2)
        if place:
            close_step(place - 1)
        if place == 0:
            w_total()
    close_step(3)

    for piece, scale in enumerate(piece_columns(scale_ref, 2 * row, SCATTER_PIECES)):
        grad_ref[pl.ds(piece * scale.shape[0], scale.shape[0]), :] = total[z, piece] * scale
    for distance in range(1, 16):
        all_arrived(distance)
    for part in range(16):
        wgrad_ref[part * 8 : part * 8 + 8, :] = w_all[part, 0:8, :]
    bgrad_ref[...] = w_all[0, 8:9, :]
    for place in range(4):
        send_step(place)
    for distance in range(1, 16):
        w_copy(distance).wait_send()
        all_copy(distance).wait_send()


def scatter_gradients(count, info, tiles, pairs, wsum, src_scale):
    dma = pltpu.SemaphoreType.DMA
    block = block_of(SCATTER_PIECES)
    return pl.pallas_call(
        scatter_kernel,
        in_specs=[pl.BlockSpec(memory_space=pltpu.SMEM)] * 2 + [VMEM_SPEC] * 4,
        out_specs=[VMEM_SPEC] * 3,
        out_shape=[
            jax.ShapeDtypeStruct((2 * TILE, TILE), F32),
            jax.ShapeDtypeStruct((TILE, TILE), F32),
            jax.ShapeDtypeStruct((1, TILE), F32),
        ],
        scratch_shapes=[pltpu.VMEM(tiles.shape, F32), pltpu.VMEM((16,) + block, F32)]
        + [pltpu.VMEM((4,) + block, F32)] * 7
        + [
            pltpu.VMEM((16,) + SLICE, F32),
            pltpu.VMEM((16,) + SLICE, F32),
            dma((4, SCATTER_PIECES)), dma((4, SCATTER_PIECES)), dma((4, 2, SCATTER_PIECES)), dma((4, 2, SCATTER_PIECES)),
            dma((4, SCATTER_PIECES)), dma((4, 2, SCATTER_PIECES)), dma((15,)), dma((16,)), dma((15,)), dma((16,)),
        ],
        compiler_params=pltpu.CompilerParams(vmem_limit_bytes=LIMIT, collective_id=2, has_side_effects=True),
        name="scatter_gradients",
    )(count, info, tiles, pairs, wsum, src_scale)


def put_kernel(*refs):
    count = len(refs) // 2
    ins, outs, sems = refs[:count], refs[count : 2 * count], refs[-1]
    copies = [pltpu.make_async_copy(ins[k], outs[k], sems.at[k]) for k in range(count)]
    for copy in copies:
        copy.start()
    for copy in copies:
        copy.wait()


def put_out(*arrays):
    return pl.pallas_call(
        put_kernel,
        in_specs=[VMEM_SPEC] * len(arrays),
        out_specs=[pl.BlockSpec(memory_space=pltpu.HBM)] * len(arrays),
        out_shape=[jax.ShapeDtypeStruct(array.shape, array.dtype) for array in arrays],
        scratch_shapes=[pltpu.SemaphoreType.DMA((len(arrays),))],
        compiler_params=pltpu.CompilerParams(vmem_limit_bytes=LIMIT),
        name="put_out",
    )(*arrays)


def local(features, weight, bias_vector, out_grad, adj_tiles, tile_slots, tile_counts):
    tiles, pairs, src_scale, dst_scale, forward_info, backward_info = gather_features(
        features, adj_tiles[0, 0], tile_slots[0], tile_counts
    )
    activated, grad_pairs, wsum = dense_layer(
        tile_counts, forward_info, tiles, pairs, weight, bias_vector, out_grad, dst_scale
    )
    feature_grad, weight_grad, bias_grad = scatter_gradients(
        tile_counts, backward_info, tiles, grad_pairs, wsum, src_scale
    )
    activated, feature_grad, weight_grad, bias_grad = put_out(activated, feature_grad, weight_grad, bias_grad)
    return activated, feature_grad, weight_grad, bias_grad.reshape(TILE)


def solution(mesh):
    return jax.shard_map(
        local,
        mesh=mesh,
        in_specs=(
            P(("col", "row"), None),
            P(),
            P(),
            P(("row", "col"), None),
            P("row", "col", None, None, None),
            P("row", "col", None),
            P("row", "col"),
        ),
        out_specs=(P(("row", "col"), None), P(("col", "row"), None), P(), P()),
        check_vma=False,
    )
```
